256 devices in a mesh: sector: 16 (over x, y_hi, core), term: 16 (over y_lo, z).
Axes of the slice: x: 4, y: 4 (y_hi: 2, y_lo: 2; y = y_hi * 2 + y_lo), z: 8, core: 2. Of those that a mesh axis runs over, the one named last changes fastest.
Arguments:
- x_start: float32 [16, 384, 384], P('sector', 'term'), may hold values from -6 to 6
- x_prev: float32 [16, 384, 384], P('sector', 'term'), may hold values from -6 to 6
- precond: float32 [16, 384, 384], P('sector', 'term'), may hold values from 0.5 to 6
- left_env: bfloat16 [2048, 384, 384], P(('sector', 'term')), may hold values from -0.20412415 to 1.2041241
- right_env: bfloat16 [2048, 384, 384], P(('sector', 'term')), may hold values from -0.20412415 to 1.2041241
- triples: int32 [5120, 4], P(('sector', 'term')), may hold values from 0 to 63, as said below
- trip_count: int32 [16, 16], P('sector', 'term'), may hold values from 5 to 20, as said below
- term_coef: float32 [64], replicated, may hold values from 0.25 to 1
- lanczos_beta: float32 [3], replicated, may hold values from 0.3 to 1.2
- block_owner: int32 [16], replicated, may hold values from 0 to 15, each once
Outputs:
- final_vector: float32 [16, 384, 384], P('sector', 'term')
- rayleigh: float32 [3], replicated
The draws below stay inside these ranges and needn't reach their ends.
Inputs may be any that keep to these rules, and one draw needn't show every extreme that they name: `triples`: Columns: a left slot below 8, a wavefunction block id below 16, a right slot below 8, an operator term below 64. `trip_count`: some device has exactly 20 live triples in every draw. `block_owner`: each sector index holds exactly one block.
All inputs are finite; a program needn't handle non-finite values.
Results may differ from the reference program's by a relative error of at most 0.006.
Values may be sent and summed in bfloat16 or wider, within the bound.
A program may use at most 64 MiB of HBM per device.

```python
import math
import jax
import jax.numpy as jnp
from jax import lax

B = 384
TRIP = 20
ENV_DEV = 8
TERMS = 64
APPS = 3
WBLK = 16
N_SECTOR = 16
N_TERM = 16


def draw_precond(key, part):
    base = jax.random.uniform(key, (N_SECTOR, B, B), jnp.float32)
    local = jnp.exp(jnp.log(0.5) + base * jnp.log(4.0))
    rising = 1.0 + 2.0 * jnp.arange(N_SECTOR, dtype=jnp.float32) / max(N_SECTOR - 1, 1)
    return local * rising[:, None, None]


def identity_blocks(count):
    rows = jnp.arange(B, dtype=jnp.int32)
    single = jnp.where(rows[:, None] == rows[None, :], 1.0, 0.0).astype(jnp.float32)
    return jnp.broadcast_to(single[None], (count, B, B))


def draw_left_env(key, part):
    count = N_SECTOR * N_TERM * ENV_DEV
    spread = 1.0 / math.sqrt(B)
    inner = jax.random.fold_in(key, 31)
    noise = jnp.clip(jax.random.normal(inner, (count, B, B), jnp.float32), -3.0, 3.0) * spread
    return (identity_blocks(count) + noise).astype(jnp.bfloat16)


def draw_right_env(key, part):
    count = N_SECTOR * N_TERM * ENV_DEV
    spread = 1.0 / math.sqrt(B)
    inner = jax.random.fold_in(key, 32)
    noise = jnp.clip(jax.random.normal(inner, (count, B, B), jnp.float32), -3.0, 3.0) * spread
    return (identity_blocks(count) + noise).astype(jnp.bfloat16)


def draw_triples(key, part):
    total_rows = N_SECTOR * N_TERM * TRIP
    left_slot = jax.random.randint(jax.random.fold_in(key, 11), (total_rows,), 0, ENV_DEV)
    wave_block = jax.random.randint(jax.random.fold_in(key, 12), (total_rows,), 0, N_SECTOR)
    right_slot = jax.random.randint(jax.random.fold_in(key, 13), (total_rows,), 0, ENV_DEV)
    term_index = jax.random.randint(jax.random.fold_in(key, 14), (total_rows,), 0, TERMS)
    return jnp.stack([left_slot, wave_block, right_slot, term_index], axis=1).astype(jnp.int32)


def draw_trip_count(key, part):
    lowest = max(1, TRIP // 4)
    spread = TRIP - lowest
    first = jax.random.randint(jax.random.fold_in(key, 21), (N_SECTOR, N_TERM), 0, spread + 1)
    second = jax.random.randint(jax.random.fold_in(key, 22), (N_SECTOR, N_TERM), 0, spread + 1)
    counts = lowest + first * second // max(spread, 1)
    pick_sector = jax.random.randint(jax.random.fold_in(key, 23), (), 0, N_SECTOR)
    pick_term = jax.random.randint(jax.random.fold_in(key, 24), (), 0, N_TERM)
    counts = counts.at[pick_sector, pick_term].set(TRIP)
    return counts.astype(jnp.int32)


def shard_levels(own_key, extent, shards, least, high):
    def one(dim, shards_of):
        steps = jax.random.uniform(jax.random.fold_in(jax.random.fold_in(own_key, 6), dim), (shards_of,), jnp.float32, least / len(shards), high / len(shards))
        return jnp.repeat(jnp.exp(steps), extent[dim] // shards_of).reshape((-1,) + (1,) * (len(extent) - dim - 1))

    level = one(*shards[0])
    for cut in shards[1:]:
        level = level * one(*cut)
    return level


def centred(key, shape, width, limit, shards=(), held_as=jnp.bfloat16):
    drawn = width * jax.random.normal(key, shape, jnp.float32)
    if shards:
        drawn = drawn * shard_levels(key, shape, shards, -0.22, 0.18)
    return jnp.clip(drawn, -limit, limit).astype(held_as)


def setup_inputs(seed: int = 0) -> dict:
    seeds = jax.random.split(jax.random.key(seed), 11)
    x_start = centred(seeds[0], (WBLK, B, B), 1.0, 6.0, ((0, 16), (1, 16)), jnp.float32)
    x_prev = centred(seeds[1], (WBLK, B, B), 1.0, 6.0, ((0, 16), (1, 16)), jnp.float32)
    precond = draw_precond(jax.random.fold_in(seeds[10], 71), 0)
    left_env = draw_left_env(jax.random.fold_in(seeds[10], 71), 0)
    right_env = draw_right_env(jax.random.fold_in(seeds[10], 71), 0)
    triples = draw_triples(jax.random.fold_in(seeds[10], 71), 0)
    trip_count = draw_trip_count(jax.random.fold_in(seeds[10], 71), 0)
    term_coef = jnp.clip(jax.random.uniform(seeds[7], (TERMS,), jnp.float32, 0.25, 1.0), 0.25, 1.0)
    lanczos_beta = jnp.clip(jax.random.uniform(seeds[8], (APPS,), jnp.float32, 0.3, 1.2), 0.3, 1.2)
    block_owner = jax.random.permutation(seeds[9], WBLK).astype(jnp.int32)
    return dict(x_start=x_start, x_prev=x_prev, precond=precond, left_env=left_env, right_env=right_env, triples=triples, trip_count=trip_count, term_coef=term_coef, lanczos_beta=lanczos_beta, block_owner=block_owner)


EPSILON = 1e-06

def reference(x_start, x_prev, precond, left_env, right_env, triples, trip_count, term_coef, lanczos_beta, block_owner):
    normaliser = 1.0 / math.sqrt(N_TERM * TRIP)
    per_sector = N_TERM * TRIP
    left_sector = left_env.reshape(N_SECTOR, N_TERM * ENV_DEV, B, B)
    right_sector = right_env.reshape(N_SECTOR, N_TERM * ENV_DEV, B, B)
    triple_rows = triples.reshape(N_SECTOR, per_sector, 4)
    slot_index = jnp.arange(per_sector, dtype=jnp.int32)
    slot_term = slot_index // TRIP
    is_live = (slot_index % TRIP)[None, :] < jnp.repeat(trip_count, TRIP, axis=1)
    weights_live = jnp.where(is_live, term_coef[triple_rows[:, :, 3]], jnp.zeros((), term_coef.dtype))

    def apply_hamiltonian(wave):

        def sector_image(operands):
            left_blocks, right_blocks, rows_here, coef_here = operands
            left_index = (slot_term * ENV_DEV + rows_here[:, 0]).astype(jnp.int32)
            right_index = (slot_term * ENV_DEV + rows_here[:, 2]).astype(jnp.int32)
            left_taken = left_blocks[left_index].astype(jnp.float32)
            wave_taken = wave[block_owner[rows_here[:, 1]]].astype(jnp.float32)
            middle = jnp.einsum('kij,kjl->kil', left_taken, wave_taken, precision=lax.Precision.HIGHEST)
            middle = lax.optimization_barrier(middle.astype(jnp.bfloat16)).astype(jnp.float32)
            right_taken = right_blocks[right_index].astype(jnp.float32)
            return jnp.einsum('kil,klm->im', middle * coef_here[:, None, None], right_taken, precision=lax.Precision.HIGHEST)
        return lax.map(sector_image, (left_sector, right_sector, triple_rows, weights_live)) * normaliser
    current, previous = (x_start, x_prev)
    quotients = []
    for position in range(APPS):
        applied = apply_hamiltonian(current.astype(jnp.bfloat16))
        quotient = jnp.sum(current * applied) / jnp.sum(current * current)
        residual = applied - quotient * current - lanczos_beta[position] * previous
        scaled = precond * residual
        following = scaled / jnp.sqrt(jnp.mean(scaled * scaled) + EPSILON)
        previous, current = (current, following)
        quotients.append(quotient)
    return (current, jnp.stack(quotients))
```

```python
import functools
import math

import jax
import jax.numpy as jnp
from jax import lax
from jax.experimental import pallas as pl
from jax.experimental.pallas import tpu as pltpu
from jax.sharding import Mesh
from jax.sharding import PartitionSpec as P

APPS = 3
B = 384
TRIP = 20
SHARE = 24
PIECE = 192
HALF = 96
GROUP = 4
SECTOR = ("x", "yh", "c")
TERM = ("yl", "z")
ALL = ("x", "yh", "c", "yl", "z")
EPSILON = 1e-06
MESH = pl.DeviceIdType.MESH
OFFSETS = (0, -1, 1, 2)


def kernel(
    x_ref,
    xp_ref,
    d_ref,
    left_hbm,
    right_hbm,
    triples,
    count,
    coef,
    beta,
    owner,
    out_ref,
    ray_ref,
    left,
    right,
    wave,
    mid,
    img,
    pimg,
    rsbuf,
    zimg,
    zcur,
    zprev,
    zdiag,
    cur,
    prev,
    sabuf,
    sbbuf,
    env_sem,
    g_send,
    g_recv,
    b_send,
    b_recv,
    r_send,
    r_recv,
    sa_send,
    sa_recv,
    sb_send,
    sb_recv,
    z_send,
    z_recv,
    i_send,
    i_recv,
):
    x = lax.axis_index("x")
    yh = lax.axis_index("yh")
    c = lax.axis_index("c")
    yl = lax.axis_index("yl")
    z = lax.axis_index("z")
    y = yh * 2 + yl
    sector = (x * 2 + yh) * 2 + c
    term = yl * 8 + z
    p = (1 - c) * y + c * x
    q = (1 - c) * x + c * y

    def device(nx, ny, nc, nz):
        return {"x": nx, "yh": ny // 2, "c": nc, "yl": ny % 2, "z": nz}

    def along_p(d):
        return device((x + c * d + 4) % 4, (y + (1 - c) * d + 4) % 4, c, z)

    def along_q(d):
        return device((x + (1 - c) * d + 4) % 4, (y + c * d + 4) % 4, c, z)

    def term_peer(dyl, dz):
        return {"x": x, "yh": yh, "c": c, "yl": (yl + dyl) % 2, "z": (z + dz) % 8}

    def sector_peer(dx, dyh, dc):
        return {"x": (x + dx) % 4, "yh": (yh + dyh) % 2, "c": (c + dc) % 2, "yl": yl, "z": z}

    term_offsets = [(o // 8, o % 8) for o in range(1, 16)]
    sector_offsets = [(o // 4, (o // 2) % 2, o % 2) for o in range(1, 16)]
    sibling = sector_peer(0, 0, 1)

    def remote(src, dst, send, recv, dev):
        return pltpu.make_async_remote_copy(
            src_ref=src, dst_ref=dst, send_sem=send, recv_sem=recv, device_id=dev, device_id_type=MESH
        )

    env = [
        pltpu.make_async_copy(left_hbm, left, env_sem.at[0]),
        pltpu.make_async_copy(right_hbm, right, env_sem.at[1]),
    ]
    for e in env:
        e.start()

    barrier = pltpu.get_barrier_semaphore()
    peers = [term_peer(*o) for o in term_offsets] + [sector_peer(*o) for o in sector_offsets]
    peers.append({"x": x, "yh": 1 - yh, "c": c, "yl": 1 - yl, "z": z})
    for dev in peers:
        pl.semaphore_signal(barrier, inc=1, device_id=dev, device_id_type=MESH)
    my_rows = pl.ds(pl.multiple_of(SHARE * term, 8), SHARE)
    cur[...] = x_ref[0]
    prev[...] = xp_ref[0]
    zcur[z] = x_ref[0]
    zprev[z] = xp_ref[0]
    zdiag[z] = d_ref[0]
    zimg[z] = x_ref[0].astype(jnp.bfloat16)
    pl.semaphore_wait(barrier, len(peers))

    def z_copy(dz):
        mine = zimg.at[z]
        return remote(mine, mine, z_send.at[dz], z_recv.at[dz], term_peer(0, dz))

    def z_arrival(dz):
        theirs = zimg.at[(z - dz + 8) % 8]
        return remote(theirs, theirs, z_send.at[dz], z_recv.at[dz], term_peer(0, dz))

    def state_copy(n, ref, dz):
        mine = ref.at[z]
        return remote(mine, mine, i_send.at[n, dz], i_recv.at[n, dz], term_peer(0, dz))

    def state_arrival(n, ref, dz):
        theirs = ref.at[(z - dz + 8) % 8]
        return remote(theirs, theirs, i_send.at[n, dz], i_recv.at[n, dz], term_peer(0, dz))

    states = ((0, zcur), (1, zprev), (2, zdiag))
    for dz in range(1, 8):
        z_copy(dz).start()
    for n, ref in states:
        for dz in range(1, 8):
            state_copy(n, ref, dz).start()
    for dz in range(1, 8):
        z_copy(dz).wait_send()
        z_arrival(dz).wait_recv()

    def set_wave(value):
        rows = pl.ds(pl.multiple_of(PIECE * yl, 64), PIECE)
        wave[sector, rows, :] = value.reshape(PIECE, B).astype(jnp.bfloat16)

    set_wave(zimg[...].astype(jnp.float32))

    def piece_at(px, py, core, start, length):
        block = (px * 2 + py // 2) * 2 + core
        rows = pl.multiple_of((py % 2) * PIECE + start, 32)
        return wave.at[block, pl.ds(rows, length)]

    def piece(a, b, start=0, length=PIECE):
        a, b = (a + 4) % 4, (b + 4) % 4
        return piece_at((1 - c) * b + c * a, (1 - c) * a + c * b, c, start, length)

    def p_copy(k):
        where = (piece(p, q), piece(p, q), piece(p - 1, q, 0, HALF), piece(p + 1, q, HALF, HALF))[k]
        dev = along_p(1 if k % 2 == 0 else -1)
        return remote(where, where, g_send.at[k], g_recv.at[k], dev)

    def p_arrival(k):
        where = (piece(p - 1, q), piece(p + 1, q), piece(p - 2, q, 0, HALF), piece(p + 2, q, HALF, HALF))[k]
        dev = along_p(1 if k % 2 == 0 else -1)
        return remote(where, where, g_send.at[k], g_recv.at[k], dev)

    def q_copy(j, k):
        a = p + OFFSETS[j]
        where = (piece(a, q), piece(a, q), piece(a, q - 1, 0, HALF), piece(a, q + 1, HALF, HALF))[k]
        dev = along_q(1 if k % 2 == 0 else -1)
        n = 4 + 4 * j + k
        return remote(where, where, g_send.at[n], g_recv.at[n], dev)

    def q_arrival(j, k):
        a = p + OFFSETS[j]
        where = (piece(a, q - 1), piece(a, q + 1), piece(a, q - 2, 0, HALF), piece(a, q + 2, HALF, HALF))[k]
        dev = along_q(1 if k % 2 == 0 else -1)
        n = 4 + 4 * j + k
        return remote(where, where, g_send.at[n], g_recv.at[n], dev)

    def to_sibling(a, b):
        a, b = (a + 4) % 4, (b + 4) % 4
        px, py = (1 - c) * b + c * a, (1 - c) * a + c * b
        where = piece_at(px, py, c, 0, PIECE)
        n = px * 4 + py
        return remote(where, where, b_send.at[n], b_recv.at[n], sibling)

    def from_sibling(n):
        where = piece_at(n // 4, n % 4, 1 - c, 0, PIECE)
        return remote(where, where, b_send.at[n], b_recv.at[n], sibling)

    def sent_to_sibling(n):
        where = piece_at(n // 4, n % 4, c, 0, PIECE)
        return remote(where, where, b_send.at[n], b_recv.at[n], sibling)

    def gather():
        p_copy(0).start()
        p_copy(1).start()
        q_copy(0, 0).start()
        q_copy(0, 1).start()
        to_sibling(p, q).start()
        for k in (0, 1):
            p_arrival(k).wait_recv()
            p_copy(2 + k).start()
        for j in (1, 2):
            q_copy(j, 0).start()
            q_copy(j, 1).start()
            to_sibling(p + OFFSETS[j], q).start()

        def neighbours(j):
            for k in (0, 1):
                q_arrival(j, k).wait_recv()
                q_copy(j, 2 + k).start()
            to_sibling(p + OFFSETS[j], q - 1).start()
            to_sibling(p + OFFSETS[j], q + 1).start()

        neighbours(0)
        p_arrival(2).wait_recv()
        p_arrival(3).wait_recv()
        q_copy(3, 0).start()
        q_copy(3, 1).start()
        to_sibling(p + 2, q).start()

        def opposite(j):
            q_arrival(j, 2).wait_recv()
            q_arrival(j, 3).wait_recv()
            to_sibling(p + OFFSETS[j], q + 2).start()

        neighbours(1)
        neighbours(2)
        opposite(0)
        neighbours(3)
        opposite(1)
        opposite(2)
        opposite(3)
        for k in range(4):
            p_copy(k).wait_send()
        for j in range(4):
            for k in range(4):
                q_copy(j, k).wait_send()
        for n in range(16):
            from_sibling(n).wait_recv()
        for n in range(16):
            sent_to_sibling(n).wait_send()

    live = count[0, 0]
    normaliser = 1.0 / math.sqrt(16 * TRIP)

    def compute():
        img[...] = jnp.zeros_like(img)

        def step(g, carry):
            for j in range(GROUP):
                k = g * GROUP + j
                weight = jnp.where(k < live, coef[triples[k, 3]] * normaliser, 0.0)
                m = jnp.dot(
                    left[triples[k, 0]], wave[owner[triples[k, 1]]], preferred_element_type=jnp.float32
                )
                mid[:, j * B : (j + 1) * B] = (m * weight).astype(jnp.bfloat16)
            rights = jnp.concatenate([right[triples[g * GROUP + j, 2]] for j in range(GROUP)], axis=0)
            img[...] += jnp.dot(mid[...], rights, preferred_element_type=jnp.float32)
            return carry

        lax.fori_loop(0, TRIP // GROUP, step, 0)
        pimg[...] = img[...].reshape(16, SHARE, B).astype(jnp.bfloat16)

    def index_of(dyl, dz):
        return dyl * 8 + dz

    def rs_copy(dyl, dz):
        to = ((yl + dyl) % 2) * 8 + (z + dz) % 8
        o = index_of(dyl, dz)
        return remote(pimg.at[to], rsbuf.at[term], r_send.at[o], r_recv.at[o], term_peer(dyl, dz))

    def rs_arrival(dyl, dz):
        sender = ((yl + dyl) % 2) * 8 + (z - dz + 8) % 8
        o = index_of(dyl, dz)
        return remote(rsbuf.at[sender], rsbuf.at[sender], r_send.at[o], r_recv.at[o], term_peer(dyl, dz))

    def sa_copy(dyl, dz):
        o = index_of(dyl, dz)
        mine = sabuf.at[term]
        return remote(mine, mine, sa_send.at[o], sa_recv.at[o], term_peer(dyl, dz))

    def sa_arrival(dyl, dz):
        o = index_of(dyl, dz)
        theirs = sabuf.at[((yl + dyl) % 2) * 8 + (z - dz + 8) % 8]
        return remote(theirs, theirs, sa_send.at[o], sa_recv.at[o], term_peer(dyl, dz))

    def sb_copy(dx, dyh, dc):
        o = dx * 4 + dyh * 2 + dc
        mine = sbbuf.at[sector]
        return remote(mine, mine, sb_send.at[o], sb_recv.at[o], sector_peer(dx, dyh, dc))

    def sb_arrival(dx, dyh, dc):
        o = dx * 4 + dyh * 2 + dc
        theirs = sbbuf.at[(((x - dx + 4) % 4) * 2 + (yh + dyh) % 2) * 2 + (c + dc) % 2]
        return remote(theirs, theirs, sb_send.at[o], sb_recv.at[o], sector_peer(dx, dyh, dc))

    for e in env:
        e.wait()

    def application(i, carry):
        gather()
        compute()
        for o in term_offsets:
            rs_copy(*o).start()
        rsbuf[term] = jnp.zeros((SHARE, B), jnp.bfloat16)
        for o in term_offsets:
            rs_arrival(*o).wait_recv()
        for o in term_offsets:
            rs_copy(*o).wait_send()
        image = img[my_rows, :]
        for t in range(16):
            image = image + rsbuf[t].astype(jnp.float32)
        now = cur[...]
        before = prev[...]
        square = d_ref[0] * d_ref[0]
        weighted = square * image
        weighted_now = square * now
        products = (
            now * image,
            now * now,
            weighted * image,
            weighted * now,
            weighted * before,
            weighted_now * now,
            weighted_now * before,
            square * before * before,
        )

        def lanes(value):
            rows = jnp.sum(value, axis=0, keepdims=True)
            return rows[:, :128] + rows[:, 128:256] + rows[:, 256:]

        sabuf[term] = jnp.concatenate([lanes(v) for v in products], axis=0)
        for o in term_offsets:
            sa_copy(*o).start()

        @pl.when(i < APPS - 1)
        def _():
            zimg[z] = image.astype(jnp.bfloat16)
            for dz in range(1, 8):
                z_copy(dz).start()

        for o in term_offsets:
            sa_arrival(*o).wait_recv()
        sbbuf[sector] = jnp.sum(sabuf[...], axis=0)
        for o in sector_offsets:
            sb_copy(*o).start()
        for o in sector_offsets:
            sb_arrival(*o).wait_recv()
        for o in term_offsets:
            sa_copy(*o).wait_send()
        for o in sector_offsets:
            sb_copy(*o).wait_send()
        totals = jnp.sum(jnp.sum(sbbuf[...], axis=0), axis=1, keepdims=True)
        cross, self_, ii, ic, ip, cc, cp, pp = [totals[j : j + 1] for j in range(8)]
        beta_now = beta[i]
        quotient = cross / self_
        squares = (
            ii
            - 2.0 * quotient * ic
            - 2.0 * beta_now * ip
            + quotient * quotient * cc
            + 2.0 * quotient * beta_now * cp
            + beta_now * beta_now * pp
        )
        inverse = 1.0 / jnp.sqrt(squares / (16 * B * B) + EPSILON)
        ray_ref[i] = jnp.sum(quotient)

        @pl.when(i < APPS - 1)
        def _():
            @pl.when(i == 0)
            def _():
                for n, ref in states:
                    for dz in range(1, 8):
                        state_arrival(n, ref, dz).wait_recv()
                        state_copy(n, ref, dz).wait_send()

            for dz in range(1, 8):
                z_arrival(dz).wait_recv()
                z_copy(dz).wait_send()
            znow = zcur[...]
            znext = zdiag[...] * (zimg[...].astype(jnp.float32) - quotient * znow - beta_now * zprev[...]) * inverse
            zprev[...] = znow
            zcur[...] = znext
            set_wave(znext)

        following = d_ref[0] * (image - quotient * now - beta_now * before) * inverse
        prev[...] = now
        cur[...] = following
        return carry

    lax.fori_loop(0, APPS, application, 0)
    out_ref[0] = cur[...]


def local(x_start, x_prev, precond, left_env, right_env, triples, trip_count, term_coef, lanczos_beta, block_owner):
    vmem = pl.BlockSpec(memory_space=pltpu.VMEM)
    smem = pl.BlockSpec(memory_space=pltpu.SMEM)
    hbm = pl.BlockSpec(memory_space=pl.ANY)
    dma = pltpu.SemaphoreType.DMA
    f32, bf16 = jnp.float32, jnp.bfloat16
    return pl.pallas_call(
        kernel,
        out_shape=(jax.ShapeDtypeStruct((1, SHARE, B), f32), jax.ShapeDtypeStruct((APPS,), f32)),
        in_specs=[vmem, vmem, vmem, hbm, hbm, smem, smem, smem, smem, smem],
        out_specs=(vmem, smem),
        scratch_shapes=[
            pltpu.VMEM((8, B, B), bf16),
            pltpu.VMEM((8, B, B), bf16),
            pltpu.VMEM((16, B, B), bf16),
            pltpu.VMEM((B, GROUP * B), bf16),
            pltpu.VMEM((B, B), f32),
            pltpu.VMEM((16, SHARE, B), bf16),
            pltpu.VMEM((16, SHARE, B), bf16),
            pltpu.VMEM((8, SHARE, B), bf16),
            pltpu.VMEM((8, SHARE, B), f32),
            pltpu.VMEM((8, SHARE, B), f32),
            pltpu.VMEM((8, SHARE, B), f32),
            pltpu.VMEM((SHARE, B), f32),
            pltpu.VMEM((SHARE, B), f32),
            pltpu.VMEM((16, 8, 128), f32),
            pltpu.VMEM((16, 8, 128), f32),
            dma((2,)),
            dma((20,)),
            dma((20,)),
            dma((16,)),
            dma((16,)),
            dma((16,)),
            dma((16,)),
            dma((16,)),
            dma((16,)),
            dma((16,)),
            dma((16,)),
            dma((8,)),
            dma((8,)),
            dma((3, 8)),
            dma((3, 8)),
        ],
        compiler_params=pltpu.CompilerParams(
            collective_id=0, has_side_effects=True, vmem_limit_bytes=48 * 2**20
        ),
        name="window",
    )(x_start, x_prev, precond, left_env, right_env, triples, trip_count, term_coef, lanczos_beta, block_owner)


def solution(mesh):
    torus = Mesh(mesh.devices.reshape(4, 2, 2, 2, 8), ALL)
    return jax.shard_map(
        local,
        mesh=torus,
        in_specs=(
            P(SECTOR, TERM, None),
            P(SECTOR, TERM, None),
            P(SECTOR, TERM, None),
            P(ALL, None, None),
            P(ALL, None, None),
            P(ALL, None),
            P(SECTOR, TERM),
            P(),
            P(),
            P(),
        ),
        out_specs=(P(SECTOR, TERM, None), P()),
        check_vma=False,
    )
```

```python
import functools
import math

import jax
import jax.numpy as jnp
from jax import lax
from jax.experimental import pallas as pl
from jax.experimental.pallas import tpu as pltpu
from jax.sharding import Mesh
from jax.sharding import PartitionSpec as P

APPS = 3
B = 384
TRIP = 20
SHARE = 24
PIECE = 192
HALF = 96
GROUP = 4
SECTOR = ("x", "yh", "c")
TERM = ("yl", "z")
ALL = ("x", "yh", "c", "yl", "z")
EPSILON = 1e-06
MESH = pl.DeviceIdType.MESH
OFFSETS = (0, -1, 1, 2)


def kernel(
    x_hbm,
    xp_hbm,
    d_hbm,
    left_hbm,
    right_hbm,
    triples_hbm,
    count_hbm,
    coef_hbm,
    beta_hbm,
    owner_hbm,
    out_ref,
    ray_ref,
    left,
    right,
    wave,
    mid,
    img,
    pimg,
    rsbuf,
    zimg,
    cur,
    prev,
    diag,
    qabuf,
    qbbuf,
    nabuf,
    nbbuf,
    triples,
    count,
    coef,
    beta,
    owner,
    in_sem,
    g_send,
    g_recv,
    b_send,
    b_recv,
    r_send,
    r_recv,
    z_send,
    z_recv,
    s_send,
    s_recv,
):
    x = lax.axis_index("x")
    yh = lax.axis_index("yh")
    c = lax.axis_index("c")
    yl = lax.axis_index("yl")
    z = lax.axis_index("z")
    y = yh * 2 + yl
    sector = (x * 2 + yh) * 2 + c
    term = yl * 8 + z
    p = (1 - c) * y + c * x
    q = (1 - c) * x + c * y

    def device(nx, ny, nc, nz):
        return {"x": nx, "yh": ny // 2, "c": nc, "yl": ny % 2, "z": nz}

    def along_p(d):
        return device((x + c * d + 4) % 4, (y + (1 - c) * d + 4) % 4, c, z)

    def along_q(d):
        return device((x + (1 - c) * d + 4) % 4, (y + c * d + 4) % 4, c, z)

    def term_peer(dyl, dz):
        return {"x": x, "yh": yh, "c": c, "yl": (yl + dyl) % 2, "z": (z + dz) % 8}

    def sector_peer(dx, dyh, dc):
        return {"x": (x + dx) % 4, "yh": (yh + dyh) % 2, "c": (c + dc) % 2, "yl": yl, "z": z}

    term_offsets = [(o // 8, o % 8) for o in range(1, 16)]
    sector_offsets = [(o // 4, (o // 2) % 2, o % 2) for o in range(1, 16)]
    sibling = sector_peer(0, 0, 1)

    def remote(src, dst, send, recv, dev):
        return pltpu.make_async_remote_copy(
            src_ref=src, dst_ref=dst, send_sem=send, recv_sem=recv, device_id=dev, device_id_type=MESH
        )

    moves = [
        pltpu.make_async_copy(src, dst, in_sem.at[n])
        for n, (src, dst) in enumerate(
            (
                (x_hbm.at[0], cur),
                (xp_hbm.at[0], prev),
                (d_hbm.at[0], diag),
                (triples_hbm, triples),
                (count_hbm, count),
                (coef_hbm, coef),
                (beta_hbm, beta),
                (owner_hbm, owner),
                (left_hbm, left),
                (right_hbm, right),
            )
        )
    ]
    for move in moves:
        move.start()

    barrier = pltpu.get_barrier_semaphore()
    peers = [term_peer(*o) for o in term_offsets] + [sector_peer(*o) for o in sector_offsets]
    peers.append({"x": x, "yh": 1 - yh, "c": c, "yl": 1 - yl, "z": z})
    for dev in peers:
        pl.semaphore_signal(barrier, inc=1, device_id=dev, device_id_type=MESH)
    my_rows = pl.ds(pl.multiple_of(SHARE * term, 8), SHARE)
    moves[0].wait()
    zimg[z] = cur[...].astype(jnp.bfloat16)
    pl.semaphore_wait(barrier, len(peers))

    def z_copy(dz):
        mine = zimg.at[z]
        return remote(mine, mine, z_send.at[dz], z_recv.at[dz], term_peer(0, dz))

    def z_arrival(dz):
        theirs = zimg.at[(z - dz + 8) % 8]
        return remote(theirs, theirs, z_send.at[dz], z_recv.at[dz], term_peer(0, dz))

    def z_start():
        for dz in range(1, 8):
            z_copy(dz).start()

    def set_wave(value):
        rows = pl.ds(pl.multiple_of(PIECE * yl, 64), PIECE)
        wave[sector, rows, :] = value.reshape(PIECE, B).astype(jnp.bfloat16)

    def piece_at(px, py, core, start, length):
        block = (px * 2 + py // 2) * 2 + core
        rows = pl.multiple_of((py % 2) * PIECE + start, 32)
        return wave.at[block, pl.ds(rows, length)]

    def piece(a, b, start=0, length=PIECE):
        a, b = (a + 4) % 4, (b + 4) % 4
        return piece_at((1 - c) * b + c * a, (1 - c) * a + c * b, c, start, length)

    def p_copy(k):
        where = (piece(p, q), piece(p, q), piece(p - 1, q, 0, HALF), piece(p + 1, q, HALF, HALF))[k]
        dev = along_p(1 if k % 2 == 0 else -1)
        return remote(where, where, g_send.at[k], g_recv.at[k], dev)

    def p_arrival(k):
        where = (piece(p - 1, q), piece(p + 1, q), piece(p - 2, q, 0, HALF), piece(p + 2, q, HALF, HALF))[k]
        dev = along_p(1 if k % 2 == 0 else -1)
        return remote(where, where, g_send.at[k], g_recv.at[k], dev)

    def q_copy(j, k):
        a = p + OFFSETS[j]
        where = (piece(a, q), piece(a, q), piece(a, q - 1, 0, HALF), piece(a, q + 1, HALF, HALF))[k]
        dev = along_q(1 if k % 2 == 0 else -1)
        n = 4 + 4 * j + k
        return remote(where, where, g_send.at[n], g_recv.at[n], dev)

    def q_arrival(j, k):
        a = p + OFFSETS[j]
        where = (piece(a, q - 1), piece(a, q + 1), piece(a, q - 2, 0, HALF), piece(a, q + 2, HALF, HALF))[k]
        dev = along_q(1 if k % 2 == 0 else -1)
        n = 4 + 4 * j + k
        return remote(where, where, g_send.at[n], g_recv.at[n], dev)

    def to_sibling(a, b):
        a, b = (a + 4) % 4, (b + 4) % 4
        px, py = (1 - c) * b + c * a, (1 - c) * a + c * b
        where = piece_at(px, py, c, 0, PIECE)
        n = px * 4 + py
        return remote(where, where, b_send.at[n], b_recv.at[n], sibling)

    def from_sibling(n):
        where = piece_at(n // 4, n % 4, 1 - c, 0, PIECE)
        return remote(where, where, b_send.at[n], b_recv.at[n], sibling)

    def sent_to_sibling(n):
        where = piece_at(n // 4, n % 4, c, 0, PIECE)
        return remote(where, where, b_send.at[n], b_recv.at[n], sibling)

    def gather(beside):
        p_copy(0).start()
        p_copy(1).start()
        q_copy(0, 0).start()
        q_copy(0, 1).start()
        to_sibling(p, q).start()
        for k in (0, 1):
            p_arrival(k).wait_recv()
            p_copy(2 + k).start()
        for j in (1, 2):
            q_copy(j, 0).start()
            q_copy(j, 1).start()
            to_sibling(p + OFFSETS[j], q).start()

        def neighbours(j):
            for k in (0, 1):
                q_arrival(j, k).wait_recv()
                q_copy(j, 2 + k).start()
            to_sibling(p + OFFSETS[j], q - 1).start()
            to_sibling(p + OFFSETS[j], q + 1).start()

        neighbours(0)
        p_arrival(2).wait_recv()
        p_arrival(3).wait_recv()
        q_copy(3, 0).start()
        q_copy(3, 1).start()
        to_sibling(p + 2, q).start()

        def opposite(j):
            q_arrival(j, 2).wait_recv()
            q_arrival(j, 3).wait_recv()
            to_sibling(p + OFFSETS[j], q + 2).start()

        neighbours(1)
        neighbours(2)
        beside()
        opposite(0)
        neighbours(3)
        opposite(1)
        opposite(2)
        opposite(3)
        for k in range(4):
            p_copy(k).wait_send()
        for j in range(4):
            for k in range(4):
                q_copy(j, k).wait_send()
        for n in range(16):
            from_sibling(n).wait_recv()
        for n in range(16):
            sent_to_sibling(n).wait_send()

    normaliser = 1.0 / math.sqrt(16 * TRIP)

    def compute():
        live = count[0]
        img[...] = jnp.zeros_like(img)

        def step(g, carry):
            for j in range(GROUP):
                k = g * GROUP + j
                weight = jnp.where(k < live, coef[triples[3, k]] * normaliser, 0.0)
                m = jnp.dot(
                    left[triples[0, k]], wave[owner[triples[1, k]]], preferred_element_type=jnp.float32
                )
                mid[:, j * B : (j + 1) * B] = (m * weight).astype(jnp.bfloat16)
            rights = jnp.concatenate([right[triples[2, g * GROUP + j]] for j in range(GROUP)], axis=0)
            img[...] += jnp.dot(mid[...], rights, preferred_element_type=jnp.float32)
            return carry

        lax.fori_loop(0, TRIP // GROUP, step, 0)

    def rs_copy(dyl, dz):
        to = ((yl + dyl) % 2) * 8 + (z + dz) % 8
        o = dyl * 8 + dz
        return remote(pimg.at[to], rsbuf.at[term], r_send.at[o], r_recv.at[o], term_peer(dyl, dz))

    def rs_arrival(dyl, dz):
        sender = ((yl + dyl) % 2) * 8 + (z - dz + 8) % 8
        o = dyl * 8 + dz
        return remote(rsbuf.at[sender], rsbuf.at[sender], r_send.at[o], r_recv.at[o], term_peer(dyl, dz))

    def spread(value):
        rows = jnp.sum(value.reshape(-1, 8, B), axis=0)
        return rows[:, :128] + rows[:, 128:256] + rows[:, 256:]

    def first_hop(buf, n, dyl, dz, arrival):
        o = dyl * 8 + dz
        slot = ((yl + dyl) % 2) * 8 + (z - dz + 8) % 8 if arrival else term
        ref = buf.at[slot]
        return remote(ref, ref, s_send.at[n, o], s_recv.at[n, o], term_peer(dyl, dz))

    def second_hop(buf, n, dx, dyh, dc, arrival):
        o = dx * 4 + dyh * 2 + dc
        slot = (((x - dx + 4) % 4) * 2 + (yh + dyh) % 2) * 2 + (c + dc) % 2 if arrival else sector
        ref = buf.at[slot]
        return remote(ref, ref, s_send.at[n, o], s_recv.at[n, o], sector_peer(dx, dyh, dc))

    def sum_start(bufs, n, value):
        bufs[0][term] = value
        for o in term_offsets:
            first_hop(bufs[0], n, *o, False).start()

    def sum_forward(bufs, n):
        for o in term_offsets:
            first_hop(bufs[0], n, *o, True).wait_recv()
        bufs[1][sector] = jnp.sum(bufs[0][...], axis=0)
        for o in sector_offsets:
            second_hop(bufs[1], n + 1, *o, False).start()

    def sum_finish(bufs, n):
        for o in sector_offsets:
            second_hop(bufs[1], n + 1, *o, True).wait_recv()
        for o in term_offsets:
            first_hop(bufs[0], n, *o, False).wait_send()
        for o in sector_offsets:
            second_hop(bufs[1], n + 1, *o, False).wait_send()
        total = jnp.sum(bufs[1][...], axis=0)
        return jnp.sum(jnp.sum(total, axis=0, keepdims=True), axis=1, keepdims=True)

    quotient_sum = (qabuf, qbbuf)
    norm_sum = (nabuf, nbbuf)

    def scale_of(total):
        return 1.0 / jnp.sqrt(total / (16 * B * B) + EPSILON)

    z_start()
    sum_start(norm_sum, 2, spread(cur[...] * cur[...]))
    for move in moves[1:]:
        move.wait()

    def application(i, carry):
        for dz in range(1, 8):
            z_arrival(dz).wait_recv()
            z_copy(dz).wait_send()
        set_wave(zimg[...].astype(jnp.float32))
        gather(functools.partial(sum_forward, norm_sum, 2))
        total = sum_finish(norm_sum, 2)
        scale = jnp.where(i == 0, 1.0, scale_of(total))
        compute()
        applied = img[...] * scale
        overlap = spread(wave[sector].astype(jnp.float32) * applied)
        sum_start(quotient_sum, 0, overlap)
        pimg[...] = applied.reshape(16, SHARE, B).astype(jnp.bfloat16)
        for o in term_offsets:
            rs_copy(*o).start()
        rsbuf[term] = jnp.zeros((SHARE, B), jnp.bfloat16)
        now = cur[...] * scale
        partial = img[my_rows, :] * scale - beta[i] * prev[...]
        prev[...] = now
        sum_forward(quotient_sum, 0)
        for o in term_offsets:
            rs_arrival(*o).wait_recv()
        for t in range(16):
            partial = partial + rsbuf[t].astype(jnp.float32)
        quotient = sum_finish(quotient_sum, 0) / (total * scale)
        residual = diag[...] * (partial - quotient * now)
        cur[...] = residual

        @pl.when(i < APPS - 1)
        def _():
            zimg[z] = residual.astype(jnp.bfloat16)
            z_start()

        sum_start(norm_sum, 2, spread(residual * residual))
        ray_ref[i] = jnp.sum(quotient)
        for o in term_offsets:
            rs_copy(*o).wait_send()
        return carry

    lax.fori_loop(0, APPS, application, 0)
    sum_forward(norm_sum, 2)
    out_ref[0] = cur[...] * scale_of(sum_finish(norm_sum, 2))


def local(x_start, x_prev, precond, left_env, right_env, triples, trip_count, term_coef, lanczos_beta, block_owner):
    vmem = pl.BlockSpec(memory_space=pltpu.VMEM)
    smem = pl.BlockSpec(memory_space=pltpu.SMEM)
    hbm = pl.BlockSpec(memory_space=pltpu.HBM)
    dma = pltpu.SemaphoreType.DMA
    f32, bf16 = jnp.float32, jnp.bfloat16
    return pl.pallas_call(
        kernel,
        out_shape=(jax.ShapeDtypeStruct((1, SHARE, B), f32), jax.ShapeDtypeStruct((APPS,), f32)),
        in_specs=[hbm] * 10,
        out_specs=(vmem, smem),
        scratch_shapes=[
            pltpu.VMEM((8, B, B), bf16),
            pltpu.VMEM((8, B, B), bf16),
            pltpu.VMEM((16, B, B), bf16),
            pltpu.VMEM((B, GROUP * B), bf16),
            pltpu.VMEM((B, B), f32),
            pltpu.VMEM((16, SHARE, B), bf16),
            pltpu.VMEM((16, SHARE, B), bf16),
            pltpu.VMEM((8, SHARE, B), bf16),
            pltpu.VMEM((SHARE, B), f32),
            pltpu.VMEM((SHARE, B), f32),
            pltpu.VMEM((SHARE, B), f32),
            pltpu.VMEM((16, 8, 128), f32),
            pltpu.VMEM((16, 8, 128), f32),
            pltpu.VMEM((16, 8, 128), f32),
            pltpu.VMEM((16, 8, 128), f32),
            pltpu.SMEM((4, TRIP), jnp.int32),
            pltpu.SMEM((1,), jnp.int32),
            pltpu.SMEM((64,), f32),
            pltpu.SMEM((APPS,), f32),
            pltpu.SMEM((16,), jnp.int32),
            dma((10,)),
            dma((20,)),
            dma((20,)),
            dma((16,)),
            dma((16,)),
            dma((16,)),
            dma((16,)),
            dma((8,)),
            dma((8,)),
            dma((4, 16)),
            dma((4, 16)),
        ],
        compiler_params=pltpu.CompilerParams(
            collective_id=0, has_side_effects=True, vmem_limit_bytes=64 * 2**20
        ),
        name="window",
    )(x_start, x_prev, precond, left_env, right_env, triples.T, trip_count.reshape(1), term_coef, lanczos_beta, block_owner)


def solution(mesh):
    torus = Mesh(mesh.devices.reshape(4, 2, 2, 2, 8), ALL)
    return jax.shard_map(
        local,
        mesh=torus,
        in_specs=(
            P(SECTOR, TERM, None),
            P(SECTOR, TERM, None),
            P(SECTOR, TERM, None),
            P(ALL, None, None),
            P(ALL, None, None),
            P(ALL, None),
            P(SECTOR, TERM),
            P(),
            P(),
            P(),
        ),
        out_specs=(P(SECTOR, TERM, None), P()),
        check_vma=False,
    )
```

```python
import math

import jax
import jax.numpy as jnp
from jax import lax
from jax.experimental import pallas as pl
from jax.experimental.pallas import tpu as pltpu
from jax.sharding import Mesh
from jax.sharding import PartitionSpec as P

APPS = 3
B = 384
TRIP = 20
SHARE = 24
PIECE = 192
HALF = 96
GROUP = 10
SECTOR = ("x", "yh", "c")
TERM = ("yl", "z")
ALL = ("x", "yh", "c", "yl", "z")
EPSILON = 1e-06
MESH = pl.DeviceIdType.MESH
OFFSETS = (0, -1, 1, 2)


def kernel(
    x_hbm,
    xp_hbm,
    d_hbm,
    left_hbm,
    right_hbm,
    triples_hbm,
    count_hbm,
    coef_hbm,
    beta_hbm,
    owner_hbm,
    out_ref,
    ray_ref,
    left,
    right,
    wave,
    mid,
    img,
    pimg,
    rsbuf,
    zimg,
    zcur,
    zprev,
    zdiag,
    scale,
    ray_now,
    cur,
    prev,
    diag,
    qabuf,
    qbbuf,
    nabuf,
    nbbuf,
    triples,
    count,
    coef,
    beta,
    owner,
    in_sem,
    g_send,
    g_recv,
    b_send,
    b_recv,
    r_send,
    r_recv,
    z_send,
    z_recv,
    s_send,
    s_recv,
    i_send,
    i_recv,
):
    x = lax.axis_index("x")
    yh = lax.axis_index("yh")
    c = lax.axis_index("c")
    yl = lax.axis_index("yl")
    z = lax.axis_index("z")
    y = yh * 2 + yl
    sector = (x * 2 + yh) * 2 + c
    term = yl * 8 + z
    p = (1 - c) * y + c * x
    q = (1 - c) * x + c * y

    def device(nx, ny, nc, nz):
        return {"x": nx, "yh": ny // 2, "c": nc, "yl": ny % 2, "z": nz}

    def along_p(d):
        return device((x + c * d + 4) % 4, (y + (1 - c) * d + 4) % 4, c, z)

    def along_q(d):
        return device((x + (1 - c) * d + 4) % 4, (y + c * d + 4) % 4, c, z)

    def term_peer(dyl, dz):
        return {"x": x, "yh": yh, "c": c, "yl": (yl + dyl) % 2, "z": (z + dz) % 8}

    def sector_peer(dx, dyh, dc):
        return {"x": (x + dx) % 4, "yh": (yh + dyh) % 2, "c": (c + dc) % 2, "yl": yl, "z": z}

    term_offsets = [(o // 8, o % 8) for o in range(1, 16)]
    sector_offsets = [(o // 4, (o // 2) % 2, o % 2) for o in range(1, 16)]
    sibling = sector_peer(0, 0, 1)

    def remote(src, dst, send, recv, dev):
        return pltpu.make_async_remote_copy(
            src_ref=src, dst_ref=dst, send_sem=send, recv_sem=recv, device_id=dev, device_id_type=MESH
        )

    moves = [
        pltpu.make_async_copy(src, dst, in_sem.at[n])
        for n, (src, dst) in enumerate(
            (
                (x_hbm.at[0], cur),
                (xp_hbm.at[0], prev),
                (d_hbm.at[0], diag),
                (triples_hbm, triples),
                (count_hbm, count),
                (coef_hbm, coef),
                (beta_hbm, beta),
                (owner_hbm, owner),
                (left_hbm, left),
                (right_hbm, right),
            )
        )
    ]
    for move in moves:
        move.start()

    barrier = pltpu.get_barrier_semaphore()
    peers = [term_peer(0, dz) for dz in range(1, 8)] + [along_p(1), along_p(-1), along_p(2)]
    peers += [along_q(1), along_q(-1), sibling]
    for dev in peers:
        pl.semaphore_signal(barrier, inc=1, device_id=dev, device_id_type=MESH)
    moves[0].wait()
    zimg[z] = cur[...].astype(jnp.bfloat16)
    scale[...] = jnp.ones_like(scale)
    pl.semaphore_wait(barrier, len(peers))

    def z_copy(dz):
        mine = zimg.at[z]
        return remote(mine, mine, z_send.at[dz], z_recv.at[dz], term_peer(0, dz))

    def z_arrival(dz):
        theirs = zimg.at[(z - dz + 8) % 8]
        return remote(theirs, theirs, z_send.at[dz], z_recv.at[dz], term_peer(0, dz))

    def z_start():
        for dz in range(1, 8):
            z_copy(dz).start()

    def set_wave(value):
        rows = pl.ds(pl.multiple_of(PIECE * yl, 64), PIECE)
        wave[sector, rows, :] = value.reshape(PIECE, B).astype(jnp.bfloat16)

    states = ((0, zcur), (1, zprev), (2, zdiag))

    def state_copy(n, dz):
        mine = states[n][1].at[z]
        return remote(mine, mine, i_send.at[n, dz], i_recv.at[n, dz], term_peer(0, dz))

    def state_arrival(n, dz):
        theirs = states[n][1].at[(z - dz + 8) % 8]
        return remote(theirs, theirs, i_send.at[n, dz], i_recv.at[n, dz], term_peer(0, dz))

    def state_start():
        for n, own in enumerate((cur, prev, diag)):
            states[n][1][z] = own[...]
            for dz in range(1, 8):
                state_copy(n, dz).start()

    def state_finish():
        for n in range(3):
            for dz in range(1, 8):
                state_arrival(n, dz).wait_recv()
                state_copy(n, dz).wait_send()

    def piece_at(px, py, core, start, length):
        block = (px * 2 + py // 2) * 2 + core
        rows = pl.multiple_of((py % 2) * PIECE + start, 32)
        return wave.at[block, pl.ds(rows, length)]

    def piece(a, b, start=0, length=PIECE):
        a, b = (a + 4) % 4, (b + 4) % 4
        return piece_at((1 - c) * b + c * a, (1 - c) * a + c * b, c, start, length)

    def p_copy(k):
        where = piece(p, q)
        return remote(where, where, g_send.at[k], g_recv.at[k], along_p((1, -1, 2)[k]))

    def p_arrival(k):
        where = piece(p - (1, -1, 2)[k], q)
        return remote(where, where, g_send.at[k], g_recv.at[k], along_p((1, -1, 2)[k]))

    def q_copy(j, k):
        a = p + OFFSETS[j]
        where = (piece(a, q), piece(a, q), piece(a, q - 1, 0, HALF), piece(a, q + 1, HALF, HALF))[k]
        dev = along_q(1 if k % 2 == 0 else -1)
        n = 4 + 4 * j + k
        return remote(where, where, g_send.at[n], g_recv.at[n], dev)

    def q_arrival(j, k):
        a = p + OFFSETS[j]
        where = (piece(a, q - 1), piece(a, q + 1), piece(a, q - 2, 0, HALF), piece(a, q + 2, HALF, HALF))[k]
        dev = along_q(1 if k % 2 == 0 else -1)
        n = 4 + 4 * j + k
        return remote(where, where, g_send.at[n], g_recv.at[n], dev)

    def to_sibling(a, b):
        a, b = (a + 4) % 4, (b + 4) % 4
        px, py = (1 - c) * b + c * a, (1 - c) * a + c * b
        where = piece_at(px, py, c, 0, PIECE)
        n = px * 4 + py
        return remote(where, where, b_send.at[n], b_recv.at[n], sibling)

    def from_sibling(n):
        where = piece_at(n // 4, n % 4, 1 - c, 0, PIECE)
        return remote(where, where, b_send.at[n], b_recv.at[n], sibling)

    def sent_to_sibling(n):
        where = piece_at(n // 4, n % 4, c, 0, PIECE)
        return remote(where, where, b_send.at[n], b_recv.at[n], sibling)

    def gather(beside):
        for k in range(3):
            p_copy(k).start()
        q_copy(0, 0).start()
        q_copy(0, 1).start()
        to_sibling(p, q).start()
        beside()

        def column(j):
            p_arrival(j - 1).wait_recv()
            q_copy(j, 0).start()
            q_copy(j, 1).start()
            to_sibling(p + OFFSETS[j], q).start()

        def neighbours(j):
            for k in (0, 1):
                q_arrival(j, k).wait_recv()
                q_copy(j, 2 + k).start()
            to_sibling(p + OFFSETS[j], q - 1).start()
            to_sibling(p + OFFSETS[j], q + 1).start()

        def opposite(j):
            q_arrival(j, 2).wait_recv()
            q_arrival(j, 3).wait_recv()
            to_sibling(p + OFFSETS[j], q + 2).start()

        column(1)
        column(2)
        neighbours(0)
        column(3)
        neighbours(1)
        neighbours(2)
        opposite(0)
        neighbours(3)
        opposite(1)
        opposite(2)
        opposite(3)
        for n in range(16):
            from_sibling(n).wait_recv()

    def gather_sent():
        for k in range(3):
            p_copy(k).wait_send()
        for j in range(4):
            for k in range(4):
                q_copy(j, k).wait_send()
        for n in range(16):
            sent_to_sibling(n).wait_send()

    normaliser = 1.0 / math.sqrt(16 * TRIP)

    def compute(rows):
        live = count[0]
        img[...] = jnp.zeros_like(img)

        def step(g, carry):
            for j in range(GROUP):
                k = g * GROUP + j
                weight = jnp.where(k < live, coef[triples[3, k]] * normaliser, 0.0)
                m = jnp.dot(
                    left[triples[0, k], rows, :],
                    wave[owner[triples[1, k]]],
                    preferred_element_type=jnp.float32,
                )
                mid[:, j * B : (j + 1) * B] = (m * weight).astype(jnp.bfloat16)
            rights = jnp.concatenate([right[triples[2, g * GROUP + j]] for j in range(GROUP)], axis=0)
            img[...] += jnp.dot(mid[...], rights, preferred_element_type=jnp.float32)
            return carry

        lax.fori_loop(0, TRIP // GROUP, step, 0)

    def rs_copy(dyl, dz):
        to = ((yl + dyl) % 2) * 8 + (z + dz) % 8
        o = dyl * 8 + dz
        return remote(pimg.at[to], rsbuf.at[term], r_send.at[o], r_recv.at[o], term_peer(dyl, dz))

    def rs_arrival(dyl, dz):
        sender = ((yl + dyl) % 2) * 8 + (z - dz + 8) % 8
        o = dyl * 8 + dz
        return remote(rsbuf.at[sender], rsbuf.at[sender], r_send.at[o], r_recv.at[o], term_peer(dyl, dz))

    def spread(value):
        rows = jnp.sum(jnp.sum(value.reshape(-1, 8, B), axis=0), axis=0, keepdims=True)
        return rows[:, :128] + rows[:, 128:256] + rows[:, 256:]

    def first_hop(buf, n, dyl, dz, arrival):
        o = dyl * 8 + dz
        slot = ((yl + dyl) % 2) * 8 + (z - dz + 8) % 8 if arrival else term
        ref = buf.at[slot]
        return remote(ref, ref, s_send.at[n, o], s_recv.at[n, o], term_peer(dyl, dz))

    def second_hop(buf, n, dx, dyh, dc, arrival):
        o = dx * 4 + dyh * 2 + dc
        slot = (((x - dx + 4) % 4) * 2 + (yh + dyh) % 2) * 2 + (c + dc) % 2 if arrival else sector
        ref = buf.at[slot]
        return remote(ref, ref, s_send.at[n, o], s_recv.at[n, o], sector_peer(dx, dyh, dc))

    def sum_start(bufs, n, value):
        bufs[0][term] = jnp.concatenate(value + [jnp.zeros((8 - len(value), 128), jnp.float32)], axis=0)
        for o in term_offsets:
            first_hop(bufs[0], n, *o, False).start()

    def sum_forward(bufs, n):
        for o in term_offsets:
            first_hop(bufs[0], n, *o, True).wait_recv()
        bufs[1][sector] = jnp.sum(bufs[0][...], axis=0)
        for o in sector_offsets:
            second_hop(bufs[1], n + 1, *o, False).start()

    def sum_finish(bufs, n):
        for o in sector_offsets:
            second_hop(bufs[1], n + 1, *o, True).wait_recv()
        return jnp.sum(jnp.sum(bufs[1][...], axis=0), axis=1, keepdims=True)

    def sum_sent(bufs, n):
        for o in term_offsets:
            first_hop(bufs[0], n, *o, False).wait_send()
        for o in sector_offsets:
            second_hop(bufs[1], n + 1, *o, False).wait_send()

    quotient_sum = (qabuf, qbbuf)
    norm_sum = (nabuf, nbbuf)

    def norm_scale(i):
        totals = sum_finish(norm_sum, 2)
        ii, ic, ip, cc, cp, pp = [totals[j : j + 1] for j in range(6)]
        quotient = ray_now[...]
        beta_now = beta[i]
        squares = (
            ii
            - 2.0 * quotient * ic
            - 2.0 * beta_now * ip
            + quotient * quotient * cc
            + 2.0 * quotient * beta_now * cp
            + beta_now * beta_now * pp
        )
        return 1.0 / jnp.sqrt(squares / (16 * B * B) + EPSILON)

    z_start()
    for move in moves[1:]:
        move.wait()
    for dz in range(1, 8):
        z_arrival(dz).wait_recv()
        z_copy(dz).wait_send()
    set_wave(zimg[...].astype(jnp.float32))
    own_rows = pl.ds(pl.multiple_of(PIECE * yl, 64), PIECE)
    other_rows = pl.ds(pl.multiple_of(PIECE * (1 - yl), 64), PIECE)
    share_rows = pl.ds(pl.multiple_of(SHARE * z, 8), SHARE)

    def application(i, carry):
        def beside():
            @pl.when(i == 0)
            def _():
                state_start()

            @pl.when(i > 0)
            def _():
                sum_forward(norm_sum, 2)

        gather(beside)

        @pl.when(i > 0)
        def _():
            scale[...] = norm_scale(i - 1)

        factor = scale[...]
        compute(other_rows)
        applied = img[...] * factor
        overlap = spread(wave[sector, other_rows, :].astype(jnp.float32) * applied)
        pimg[pl.ds((1 - yl) * 8, 8)] = applied.reshape(8, SHARE, B).astype(jnp.bfloat16)
        for dz in range(8):
            rs_copy(1, dz).start()
        gather_sent()
        compute(own_rows)
        img[...] = img[...] * factor
        applied = img[...]
        overlap = overlap + spread(wave[sector, own_rows, :].astype(jnp.float32) * applied)
        now = cur[...] * factor
        sum_start(quotient_sum, 0, [overlap * factor, spread(now * now)])
        pimg[pl.ds(yl * 8, 8)] = applied.reshape(8, SHARE, B).astype(jnp.bfloat16)
        for dz in range(1, 8):
            rs_copy(0, dz).start()
        rsbuf[term] = jnp.zeros((SHARE, B), jnp.bfloat16)

        @pl.when(i == 0)
        def _():
            state_finish()

        @pl.when(i > 0)
        def _():
            sum_sent(norm_sum, 2)
            zcur[...] = zcur[...] * factor

        before = prev[...]
        square = diag[...] * diag[...]
        squared_now = square * now
        squared_before = square * before
        fixed = [spread(squared_now * now), spread(squared_now * before), spread(squared_before * before)]
        sum_forward(quotient_sum, 0)
        for o in term_offsets:
            rs_arrival(*o).wait_recv()
        image = img[share_rows, :]
        for t in range(16):
            image = image + rsbuf[t].astype(jnp.float32)

        @pl.when(i < APPS - 1)
        def _():
            zimg[z] = image.astype(jnp.bfloat16)
            z_start()

        squared_image = square * image
        sum_start(
            norm_sum,
            2,
            [spread(squared_image * image), spread(squared_now * image), spread(squared_before * image)] + fixed,
        )
        for o in term_offsets:
            rs_copy(*o).wait_send()
        totals = sum_finish(quotient_sum, 0)
        quotient = totals[0:1] / totals[1:2]
        ray_now[...] = quotient
        beta_now = beta[i]

        @pl.when(i < APPS - 1)
        def _():
            for dz in range(1, 8):
                z_arrival(dz).wait_recv()
            znow = zcur[...]
            znext = zdiag[...] * (zimg[...].astype(jnp.float32) - quotient * znow - beta_now * zprev[...])
            set_wave(znext)
            zprev[...] = znow
            zcur[...] = znext
            for dz in range(1, 8):
                z_copy(dz).wait_send()

        cur[...] = diag[...] * (image - quotient * now - beta_now * before)
        prev[...] = now
        ray_ref[i] = jnp.sum(quotient)
        sum_sent(quotient_sum, 0)
        return carry

    lax.fori_loop(0, APPS, application, 0)
    sum_forward(norm_sum, 2)
    out_ref[0] = cur[...] * norm_scale(APPS - 1)
    sum_sent(norm_sum, 2)


def local(x_start, x_prev, precond, left_env, right_env, triples, trip_count, term_coef, lanczos_beta, block_owner):
    vmem = pl.BlockSpec(memory_space=pltpu.VMEM)
    smem = pl.BlockSpec(memory_space=pltpu.SMEM)
    hbm = pl.BlockSpec(memory_space=pltpu.HBM)
    dma = pltpu.SemaphoreType.DMA
    f32, bf16 = jnp.float32, jnp.bfloat16
    return pl.pallas_call(
        kernel,
        out_shape=(jax.ShapeDtypeStruct((1, SHARE, B), f32), jax.ShapeDtypeStruct((APPS,), f32)),
        in_specs=[hbm] * 10,
        out_specs=(vmem, smem),
        scratch_shapes=[
            pltpu.VMEM((8, B, B), bf16),
            pltpu.VMEM((8, B, B), bf16),
            pltpu.VMEM((16, B, B), bf16),
            pltpu.VMEM((PIECE, GROUP * B), bf16),
            pltpu.VMEM((PIECE, B), f32),
            pltpu.VMEM((16, SHARE, B), bf16),
            pltpu.VMEM((16, SHARE, B), bf16),
            pltpu.VMEM((8, SHARE, B), bf16),
            pltpu.VMEM((8, SHARE, B), f32),
            pltpu.VMEM((8, SHARE, B), f32),
            pltpu.VMEM((8, SHARE, B), f32),
            pltpu.VMEM((1, 1), f32),
            pltpu.VMEM((1, 1), f32),
            pltpu.VMEM((SHARE, B), f32),
            pltpu.VMEM((SHARE, B), f32),
            pltpu.VMEM((SHARE, B), f32),
            pltpu.VMEM((16, 8, 128), f32),
            pltpu.VMEM((16, 8, 128), f32),
            pltpu.VMEM((16, 8, 128), f32),
            pltpu.VMEM((16, 8, 128), f32),
            pltpu.SMEM((4, TRIP), jnp.int32),
            pltpu.SMEM((1,), jnp.int32),
            pltpu.SMEM((64,), f32),
            pltpu.SMEM((APPS,), f32),
            pltpu.SMEM((16,), jnp.int32),
            dma((10,)),
            dma((20,)),
            dma((20,)),
            dma((16,)),
            dma((16,)),
            dma((16,)),
            dma((16,)),
            dma((8,)),
            dma((8,)),
            dma((4, 16)),
            dma((4, 16)),
            dma((3, 8)),
            dma((3, 8)),
        ],
        compiler_params=pltpu.CompilerParams(
            collective_id=0, has_side_effects=True, vmem_limit_bytes=64 * 2**20
        ),
        name="window",
    )(x_start, x_prev, precond, left_env, right_env, triples.T, trip_count.reshape(1), term_coef, lanczos_beta, block_owner)


def solution(mesh):
    torus = Mesh(mesh.devices.reshape(4, 2, 2, 2, 8), ALL)
    return jax.shard_map(
        local,
        mesh=torus,
        in_specs=(
            P(SECTOR, TERM, None),
            P(SECTOR, TERM, None),
            P(SECTOR, TERM, None),
            P(ALL, None, None),
            P(ALL, None, None),
            P(ALL, None),
            P(SECTOR, TERM),
            P(),
            P(),
            P(),
        ),
        out_specs=(P(SECTOR, TERM, None), P()),
        check_vma=False,
    )
```

```python
import math

import jax
import jax.numpy as jnp
from jax import lax
from jax.experimental import pallas as pl
from jax.experimental.pallas import tpu as pltpu
from jax.sharding import Mesh
from jax.sharding import PartitionSpec as P

APPS = 3
B = 384
TRIP = 20
SHARE = 24
PIECE = 192
HALF = 96
GROUP = 10
SECTOR = ("x", "yh", "c")
TERM = ("yl", "z")
ALL = ("x", "yh", "c", "yl", "z")
EPSILON = 1e-06
MESH = pl.DeviceIdType.MESH
OFFSETS = (0, -1, 1, 2)


def kernel(
    x_hbm,
    xp_hbm,
    d_hbm,
    left_hbm,
    right_hbm,
    triples_hbm,
    count_hbm,
    coef_hbm,
    beta_hbm,
    owner_hbm,
    out_ref,
    ray_ref,
    left,
    right,
    wave,
    mid,
    img,
    pimg,
    rsbuf,
    zimg,
    zcur,
    zprev,
    zdiag,
    scale,
    ray_now,
    cur,
    prev,
    diag,
    qabuf,
    qbbuf,
    nabuf,
    nbbuf,
    triples,
    count,
    coef,
    beta,
    owner,
    in_sem,
    g_send,
    g_recv,
    q_send,
    b_send,
    b_recv,
    r_send,
    r_recv,
    z_send,
    z_recv,
    s_send,
    s_recv,
    i_send,
    i_recv,
):
    x = lax.axis_index("x")
    yh = lax.axis_index("yh")
    c = lax.axis_index("c")
    yl = lax.axis_index("yl")
    z = lax.axis_index("z")
    y = yh * 2 + yl
    sector = (x * 2 + yh) * 2 + c
    term = yl * 8 + z
    p = (1 - c) * y + c * x
    q = (1 - c) * x + c * y

    def device(nx, ny, nc, nz):
        return {"x": nx, "yh": ny // 2, "c": nc, "yl": ny % 2, "z": nz}

    def along_p(d):
        return device((x + c * d + 4) % 4, (y + (1 - c) * d + 4) % 4, c, z)

    def along_q(d):
        return device((x + (1 - c) * d + 4) % 4, (y + c * d + 4) % 4, c, z)

    def term_peer(dyl, dz):
        return {"x": x, "yh": yh, "c": c, "yl": (yl + dyl) % 2, "z": (z + dz) % 8}

    def sector_peer(dx, dyh, dc):
        return {"x": (x + dx) % 4, "yh": (yh + dyh) % 2, "c": (c + dc) % 2, "yl": yl, "z": z}

    term_offsets = [(o // 8, o % 8) for o in range(1, 16)]
    sector_offsets = [(o // 4, (o // 2) % 2, o % 2) for o in range(1, 16)]
    sibling = sector_peer(0, 0, 1)

    def remote(src, dst, send, recv, dev):
        return pltpu.make_async_remote_copy(
            src_ref=src, dst_ref=dst, send_sem=send, recv_sem=recv, device_id=dev, device_id_type=MESH
        )

    moves = [
        pltpu.make_async_copy(src, dst, in_sem.at[n])
        for n, (src, dst) in enumerate(
            (
                (x_hbm.at[0], cur),
                (xp_hbm.at[0], prev),
                (d_hbm.at[0], diag),
                (triples_hbm, triples),
                (count_hbm, count),
                (coef_hbm, coef),
                (beta_hbm, beta),
                (owner_hbm, owner),
                (left_hbm, left),
                (right_hbm, right),
            )
        )
    ]
    for move in moves:
        move.start()

    barrier = pltpu.get_barrier_semaphore()
    peers = [term_peer(0, dz) for dz in range(1, 8)] + [along_p(1), along_p(-1), along_p(2)]
    peers += [along_q(1), along_q(-1), sibling]
    for dev in peers:
        pl.semaphore_signal(barrier, inc=1, device_id=dev, device_id_type=MESH)
    moves[0].wait()
    zimg[z] = cur[...].astype(jnp.bfloat16)
    scale[...] = jnp.ones_like(scale)
    pl.semaphore_wait(barrier, len(peers))

    def z_copy(dz):
        mine = zimg.at[z]
        return remote(mine, mine, z_send, z_recv, term_peer(0, dz))

    def all_of(ref, length, send, recv):
        return remote(ref.at[pl.ds(0, length)], ref.at[pl.ds(0, length)], send, recv, sibling)

    z_all = all_of(zimg, 7, z_send, z_recv)

    def z_start():
        for dz in range(1, 8):
            z_copy(dz).start()

    def set_wave(value):
        rows = pl.ds(pl.multiple_of(PIECE * yl, 64), PIECE)
        wave[sector, rows, :] = value.reshape(PIECE, B).astype(jnp.bfloat16)

    states = ((0, zcur), (1, zprev), (2, zdiag))

    def state_copy(n, dz):
        mine = states[n][1].at[z]
        return remote(mine, mine, i_send.at[n], i_recv.at[n], term_peer(0, dz))

    def state_start():
        for n, own in enumerate((cur, prev, diag)):
            states[n][1][z] = own[...]
            for dz in range(1, 8):
                state_copy(n, dz).start()

    def state_finish():
        for n in range(3):
            everything = all_of(states[n][1], 7, i_send.at[n], i_recv.at[n])
            everything.wait_recv()
            everything.wait_send()

    def piece_at(px, py, core, start, length):
        block = (px * 2 + py // 2) * 2 + core
        rows = pl.multiple_of((py % 2) * PIECE + start, 32)
        return wave.at[block, pl.ds(rows, length)]

    def piece(a, b, start=0, length=PIECE):
        a, b = (a + 4) % 4, (b + 4) % 4
        return piece_at((1 - c) * b + c * a, (1 - c) * a + c * b, c, start, length)

    def p_copy(k):
        where = piece(p, q)
        return remote(where, where, g_send.at[k], g_recv.at[k], along_p((1, -1, 2)[k]))

    def p_arrival(k):
        where = piece(p - (1, -1, 2)[k], q)
        return remote(where, where, g_send.at[k], g_recv.at[k], along_p((1, -1, 2)[k]))

    def q_copy(j, k):
        a = p + OFFSETS[j]
        where = (piece(a, q), piece(a, q), piece(a, q - 1, 0, HALF), piece(a, q + 1, HALF, HALF))[k]
        dev = along_q(1 if k % 2 == 0 else -1)
        n = 3 + 4 * j + k
        if j == 3 and k == 2:
            where, dev = piece(a, q), along_q(2)
        return remote(where, where, q_send, g_recv.at[n], dev)

    def q_arrival(j, k):
        a = p + OFFSETS[j]
        where = (piece(a, q - 1), piece(a, q + 1), piece(a, q - 2, 0, HALF), piece(a, q + 2, HALF, HALF))[k]
        dev = along_q(1 if k % 2 == 0 else -1)
        n = 3 + 4 * j + k
        if j == 3 and k == 2:
            where, dev = piece(a, q - 2), along_q(2)
        return remote(where, where, q_send, g_recv.at[n], dev)

    def to_sibling(a, b):
        where = piece(a, b)
        return remote(where, where, b_send, b_recv, sibling)

    half_of_all = all_of(wave, 8, b_send, b_recv)

    def gather(beside):
        for k in range(3):
            p_copy(k).start()
        q_copy(0, 0).start()
        q_copy(0, 1).start()
        to_sibling(p, q).start()
        beside()

        def column(j):
            p_arrival(j - 1).wait_recv()
            q_copy(j, 0).start()
            q_copy(j, 1).start()
            if j == 3:
                q_copy(j, 2).start()
            to_sibling(p + OFFSETS[j], q).start()

        def neighbours(j):
            for k in (0, 1):
                q_arrival(j, k).wait_recv()
                if j < 3:
                    q_copy(j, 2 + k).start()
            to_sibling(p + OFFSETS[j], q - 1).start()
            to_sibling(p + OFFSETS[j], q + 1).start()

        def opposite(j):
            q_arrival(j, 2).wait_recv()
            if j < 3:
                q_arrival(j, 3).wait_recv()
            to_sibling(p + OFFSETS[j], q + 2).start()

        column(1)
        column(2)
        neighbours(0)
        column(3)
        neighbours(1)
        neighbours(2)
        opposite(0)
        neighbours(3)
        opposite(1)
        opposite(2)
        opposite(3)
        half_of_all.wait_recv()

    def gather_sent():
        for k in range(3):
            p_copy(k).wait_send()
        all_of(wave, 6, q_send, b_recv).wait_send()
        half_of_all.wait_send()

    normaliser = 1.0 / math.sqrt(16 * TRIP)

    def compute(rows):
        live = count[0]
        img[...] = jnp.zeros_like(img)

        def step(g, carry):
            for j in range(GROUP):
                k = g * GROUP + j
                weight = jnp.where(k < live, coef[triples[3, k]] * normaliser, 0.0)
                m = jnp.dot(
                    left[triples[0, k], rows, :],
                    wave[owner[triples[1, k]]],
                    preferred_element_type=jnp.float32,
                )
                mid[:, j * B : (j + 1) * B] = (m * weight).astype(jnp.bfloat16)
            rights = jnp.concatenate([right[triples[2, g * GROUP + j]] for j in range(GROUP)], axis=0)
            img[...] += jnp.dot(mid[...], rights, preferred_element_type=jnp.float32)
            return carry

        lax.fori_loop(0, TRIP // GROUP, step, 0)

    def rs_copy(dyl, dz):
        to = ((yl + dyl) % 2) * 8 + (z + dz) % 8
        return remote(pimg.at[to], rsbuf.at[term], r_send, r_recv, term_peer(dyl, dz))

    def spread(value):
        rows = jnp.sum(jnp.sum(value.reshape(-1, 8, B), axis=0), axis=0, keepdims=True)
        return rows[:, :128] + rows[:, 128:256] + rows[:, 256:]

    def sum_start(bufs, n, value):
        mine = bufs[0].at[term]
        mine[...] = jnp.concatenate(value + [jnp.zeros((8 - len(value), 128), jnp.float32)], axis=0)
        for o in term_offsets:
            remote(mine, mine, s_send.at[n], s_recv.at[n], term_peer(*o)).start()

    def sum_forward(bufs, n):
        all_of(bufs[0], 15, s_send.at[n], s_recv.at[n]).wait_recv()
        mine = bufs[1].at[sector]
        mine[...] = jnp.sum(bufs[0][...], axis=0)
        for o in sector_offsets:
            remote(mine, mine, s_send.at[n + 1], s_recv.at[n + 1], sector_peer(*o)).start()

    def sum_finish(bufs, n):
        all_of(bufs[1], 15, s_send.at[n + 1], s_recv.at[n + 1]).wait_recv()
        return jnp.sum(jnp.sum(bufs[1][...], axis=0), axis=1, keepdims=True)

    def sum_sent(bufs, n):
        all_of(bufs[0], 15, s_send.at[n], s_recv.at[n]).wait_send()
        all_of(bufs[1], 15, s_send.at[n + 1], s_recv.at[n + 1]).wait_send()

    quotient_sum = (qabuf, qbbuf)
    norm_sum = (nabuf, nbbuf)

    def norm_scale(i):
        totals = sum_finish(norm_sum, 2)
        ii, ic, ip, cc, cp, pp = [totals[j : j + 1] for j in range(6)]
        quotient = ray_now[...]
        beta_now = beta[i]
        squares = (
            ii
            - 2.0 * quotient * ic
            - 2.0 * beta_now * ip
            + quotient * quotient * cc
            + 2.0 * quotient * beta_now * cp
            + beta_now * beta_now * pp
        )
        return 1.0 / jnp.sqrt(squares / (16 * B * B) + EPSILON)

    z_start()
    for move in moves[1:]:
        move.wait()
    z_all.wait_recv()
    z_all.wait_send()
    set_wave(zimg[...].astype(jnp.float32))
    own_rows = pl.ds(pl.multiple_of(PIECE * yl, 64), PIECE)
    other_rows = pl.ds(pl.multiple_of(PIECE * (1 - yl), 64), PIECE)
    share_rows = pl.ds(pl.multiple_of(SHARE * z, 8), SHARE)

    def application(i, carry):
        def beside():
            @pl.when(i == 0)
            def _():
                state_start()

            @pl.when(i > 0)
            def _():
                sum_forward(norm_sum, 2)

        gather(beside)

        @pl.when(i > 0)
        def _():
            scale[...] = norm_scale(i - 1)

        factor = scale[...]
        compute(other_rows)
        applied = img[...] * factor
        overlap = spread(wave[sector, other_rows, :].astype(jnp.float32) * applied)
        pimg[pl.ds((1 - yl) * 8, 8)] = applied.reshape(8, SHARE, B).astype(jnp.bfloat16)
        for dz in range(8):
            rs_copy(1, dz).start()
        gather_sent()
        compute(own_rows)
        img[...] = img[...] * factor
        applied = img[...]
        overlap = overlap + spread(wave[sector, own_rows, :].astype(jnp.float32) * applied)
        now = cur[...] * factor
        sum_start(quotient_sum, 0, [overlap * factor, spread(now * now)])
        pimg[pl.ds(yl * 8, 8)] = applied.reshape(8, SHARE, B).astype(jnp.bfloat16)
        for dz in range(1, 8):
            rs_copy(0, dz).start()
        rsbuf[term] = jnp.zeros((SHARE, B), jnp.bfloat16)

        @pl.when(i == 0)
        def _():
            state_finish()

        @pl.when(i > 0)
        def _():
            sum_sent(norm_sum, 2)
            zcur[...] = zcur[...] * factor

        before = prev[...]
        square = diag[...] * diag[...]
        squared_now = square * now
        squared_before = square * before
        fixed = [spread(squared_now * now), spread(squared_now * before), spread(squared_before * before)]
        sum_forward(quotient_sum, 0)
        all_of(rsbuf, 15, r_send, r_recv).wait_recv()
        image = img[share_rows, :]
        for t in range(16):
            image = image + rsbuf[t].astype(jnp.float32)

        @pl.when(i < APPS - 1)
        def _():
            zimg[z] = image.astype(jnp.bfloat16)
            z_start()

        squared_image = square * image
        sum_start(
            norm_sum,
            2,
            [spread(squared_image * image), spread(squared_now * image), spread(squared_before * image)] + fixed,
        )
        all_of(pimg, 15, r_send, r_recv).wait_send()
        totals = sum_finish(quotient_sum, 0)
        quotient = totals[0:1] / totals[1:2]
        ray_now[...] = quotient
        beta_now = beta[i]

        @pl.when(i < APPS - 1)
        def _():
            z_all.wait_recv()
            znow = zcur[...]
            znext = zdiag[...] * (zimg[...].astype(jnp.float32) - quotient * znow - beta_now * zprev[...])
            set_wave(znext)
            zprev[...] = znow
            zcur[...] = znext
            z_all.wait_send()

        cur[...] = diag[...] * (image - quotient * now - beta_now * before)
        prev[...] = now
        ray_ref[i] = jnp.sum(quotient)
        sum_sent(quotient_sum, 0)
        return carry

    lax.fori_loop(0, APPS, application, 0)
    sum_forward(norm_sum, 2)
    out_ref[0] = cur[...] * norm_scale(APPS - 1)
    sum_sent(norm_sum, 2)


def local(x_start, x_prev, precond, left_env, right_env, triples, trip_count, term_coef, lanczos_beta, block_owner):
    vmem = pl.BlockSpec(memory_space=pltpu.VMEM)
    smem = pl.BlockSpec(memory_space=pltpu.SMEM)
    hbm = pl.BlockSpec(memory_space=pltpu.HBM)
    dma = pltpu.SemaphoreType.DMA
    f32, bf16 = jnp.float32, jnp.bfloat16
    return pl.pallas_call(
        kernel,
        out_shape=(jax.ShapeDtypeStruct((1, SHARE, B), f32), jax.ShapeDtypeStruct((APPS,), f32)),
        in_specs=[hbm] * 10,
        out_specs=(vmem, smem),
        scratch_shapes=[
            pltpu.VMEM((8, B, B), bf16),
            pltpu.VMEM((8, B, B), bf16),
            pltpu.VMEM((16, B, B), bf16),
            pltpu.VMEM((PIECE, GROUP * B), bf16),
            pltpu.VMEM((PIECE, B), f32),
            pltpu.VMEM((16, SHARE, B), bf16),
            pltpu.VMEM((16, SHARE, B), bf16),
            pltpu.VMEM((8, SHARE, B), bf16),
            pltpu.VMEM((8, SHARE, B), f32),
            pltpu.VMEM((8, SHARE, B), f32),
            pltpu.VMEM((8, SHARE, B), f32),
            pltpu.VMEM((1, 1), f32),
            pltpu.VMEM((1, 1), f32),
            pltpu.VMEM((SHARE, B), f32),
            pltpu.VMEM((SHARE, B), f32),
            pltpu.VMEM((SHARE, B), f32),
            pltpu.VMEM((16, 8, 128), f32),
            pltpu.VMEM((16, 8, 128), f32),
            pltpu.VMEM((16, 8, 128), f32),
            pltpu.VMEM((16, 8, 128), f32),
            pltpu.SMEM((4, TRIP), jnp.int32),
            pltpu.SMEM((1,), jnp.int32),
            pltpu.SMEM((64,), f32),
            pltpu.SMEM((APPS,), f32),
            pltpu.SMEM((16,), jnp.int32),
            dma((10,)),
            dma((3,)),
            dma((19,)),
            dma,
            dma,
            dma,
            dma,
            dma,
            dma,
            dma,
            dma((4,)),
            dma((4,)),
            dma((3,)),
            dma((3,)),
        ],
        compiler_params=pltpu.CompilerParams(
            collective_id=0, has_side_effects=True, vmem_limit_bytes=64 * 2**20
        ),
        name="window",
    )(x_start, x_prev, precond, left_env, right_env, triples.T, trip_count.reshape(1), term_coef, lanczos_beta, block_owner)


def solution(mesh):
    torus = Mesh(mesh.devices.reshape(4, 2, 2, 2, 8), ALL)
    return jax.shard_map(
        local,
        mesh=torus,
        in_specs=(
            P(SECTOR, TERM, None),
            P(SECTOR, TERM, None),
            P(SECTOR, TERM, None),
            P(ALL, None, None),
            P(ALL, None, None),
            P(ALL, None),
            P(SECTOR, TERM),
            P(),
            P(),
            P(),
        ),
        out_specs=(P(SECTOR, TERM, None), P()),
        check_vma=False,
    )
```

```python
import math

import jax
import jax.numpy as jnp
from jax import lax
from jax.experimental import pallas as pl
from jax.experimental.pallas import tpu as pltpu
from jax.sharding import Mesh
from jax.sharding import PartitionSpec as P

APPS = 3
B = 384
TRIP = 20
SHARE = 24
PIECE = 192
HALF = 96
SECTOR = ("x", "yh", "c")
TERM = ("yl", "z")
ALL = ("x", "yh", "c", "yl", "z")
EPSILON = 1e-06
MESH = pl.DeviceIdType.MESH
OFFSETS = (0, -1, 1, 2)


def kernel(
    x_hbm,
    xp_hbm,
    d_hbm,
    left_hbm,
    right_hbm,
    triples_hbm,
    count_hbm,
    coef_hbm,
    beta_hbm,
    owner_hbm,
    out_ref,
    ray_ref,
    left,
    right,
    wave,
    mid,
    img,
    pimg,
    rsbuf,
    zimg,
    zcur,
    zprev,
    zdiag,
    scale,
    ray_now,
    cur,
    prev,
    diag,
    last,
    qabuf,
    qbbuf,
    nabuf,
    nbbuf,
    triples,
    count,
    coef,
    beta,
    owner,
    in_sem,
    g_send,
    g_recv,
    q_send,
    b_send,
    b_recv,
    r_send,
    r_recv,
    z_send,
    z_recv,
    s_send,
    s_recv,
    i_send,
    i_recv,
):
    x = lax.axis_index("x")
    yh = lax.axis_index("yh")
    c = lax.axis_index("c")
    yl = lax.axis_index("yl")
    z = lax.axis_index("z")
    y = yh * 2 + yl
    sector = (x * 2 + yh) * 2 + c
    term = yl * 8 + z
    p = (1 - c) * y + c * x
    q = (1 - c) * x + c * y

    def device(nx, ny, nc, nz):
        return {"x": nx, "yh": ny // 2, "c": nc, "yl": ny % 2, "z": nz}

    def along_p(d):
        return device((x + c * d + 4) % 4, (y + (1 - c) * d + 4) % 4, c, z)

    def along_q(d):
        return device((x + (1 - c) * d + 4) % 4, (y + c * d + 4) % 4, c, z)

    def term_peer(dyl, dz):
        return {"x": x, "yh": yh, "c": c, "yl": (yl + dyl) % 2, "z": (z + dz) % 8}

    def sector_peer(dx, dyh, dc):
        return {"x": (x + dx) % 4, "yh": (yh + dyh) % 2, "c": (c + dc) % 2, "yl": yl, "z": z}

    ring = (4, 3, 5, 2, 6, 1, 7)
    term_offsets = [(1, 4), (1, 3), (1, 5), (0, 4)] + [(1, 2), (1, 6), (0, 3), (0, 5), (1, 1), (1, 7)]
    term_offsets += [(0, 2), (0, 6), (1, 0), (0, 1), (0, 7)]
    sector_offsets = [(2, 1, 0), (2, 1, 1), (1, 1, 0), (1, 1, 1), (3, 1, 0), (3, 1, 1), (2, 0, 0), (2, 0, 1)]
    sector_offsets += [(0, 1, 0), (0, 1, 1), (1, 0, 0), (1, 0, 1), (3, 0, 0), (3, 0, 1), (0, 0, 1)]
    sibling = sector_peer(0, 0, 1)

    def remote(src, dst, send, recv, dev):
        return pltpu.make_async_remote_copy(
            src_ref=src, dst_ref=dst, send_sem=send, recv_sem=recv, device_id=dev, device_id_type=MESH
        )

    moves = [
        pltpu.make_async_copy(src, dst, in_sem.at[n])
        for n, (src, dst) in enumerate(
            (
                (x_hbm.at[0], cur),
                (xp_hbm.at[0], prev),
                (d_hbm.at[0], diag),
                (triples_hbm, triples),
                (count_hbm, count),
                (coef_hbm, coef),
                (beta_hbm, beta),
                (owner_hbm, owner),
                (left_hbm, left),
                (right_hbm, right),
            )
        )
    ]
    for move in moves:
        move.start()

    barrier = pltpu.get_barrier_semaphore()
    peers = [term_peer(0, dz) for dz in ring] + [along_p(1), along_p(-1), along_p(2)]
    peers += [along_q(1), along_q(-1), sibling]
    for dev in peers:
        pl.semaphore_signal(barrier, inc=1, device_id=dev, device_id_type=MESH)
    moves[0].wait()
    zimg[z] = cur[...].astype(jnp.bfloat16)
    scale[...] = jnp.ones_like(scale)
    pl.semaphore_wait(barrier, len(peers))

    def z_copy(dz):
        mine = zimg.at[z]
        return remote(mine, mine, z_send, z_recv, term_peer(0, dz))

    def all_of(ref, length, send, recv):
        return remote(ref.at[pl.ds(0, length)], ref.at[pl.ds(0, length)], send, recv, sibling)

    z_all = all_of(zimg, 7, z_send, z_recv)

    def z_start():
        for dz in ring:
            z_copy(dz).start()

    def set_wave(value):
        rows = pl.ds(pl.multiple_of(PIECE * yl, 64), PIECE)
        wave[sector, rows, :] = value.reshape(PIECE, B).astype(jnp.bfloat16)

    states = ((0, zcur), (1, zprev), (2, zdiag))

    def state_copy(n, dz):
        mine = states[n][1].at[z]
        return remote(mine, mine, i_send.at[n], i_recv.at[n], term_peer(0, dz))

    def state_start():
        for n, own in enumerate((cur, prev, diag)):
            states[n][1][z] = own[...]
            for dz in ring:
                state_copy(n, dz).start()

    def state_finish():
        for n in range(3):
            everything = all_of(states[n][1], 7, i_send.at[n], i_recv.at[n])
            everything.wait_recv()
            everything.wait_send()

    def piece_at(px, py, core, start, length):
        block = (px * 2 + py // 2) * 2 + core
        rows = pl.multiple_of((py % 2) * PIECE + start, 32)
        return wave.at[block, pl.ds(rows, length)]

    def piece(a, b, start=0, length=PIECE):
        a, b = (a + 4) % 4, (b + 4) % 4
        return piece_at((1 - c) * b + c * a, (1 - c) * a + c * b, c, start, length)

    def p_copy(k):
        where = piece(p, q)
        return remote(where, where, g_send.at[k], g_recv.at[k], along_p((1, -1, 2)[k]))

    def p_arrival(k):
        where = piece(p - (1, -1, 2)[k], q)
        return remote(where, where, g_send.at[k], g_recv.at[k], along_p((1, -1, 2)[k]))

    def q_copy(j, k):
        a = p + OFFSETS[j]
        where = (piece(a, q), piece(a, q), piece(a, q - 1, 0, HALF), piece(a, q + 1, HALF, HALF))[k]
        dev = along_q(1 if k % 2 == 0 else -1)
        n = 3 + 4 * j + k
        if j == 3 and k == 2:
            where, dev = piece(a, q), along_q(2)
        return remote(where, where, q_send, g_recv.at[n], dev)

    def q_arrival(j, k):
        a = p + OFFSETS[j]
        where = (piece(a, q - 1), piece(a, q + 1), piece(a, q - 2, 0, HALF), piece(a, q + 2, HALF, HALF))[k]
        dev = along_q(1 if k % 2 == 0 else -1)
        n = 3 + 4 * j + k
        if j == 3 and k == 2:
            where, dev = piece(a, q - 2), along_q(2)
        return remote(where, where, q_send, g_recv.at[n], dev)

    def to_sibling(a, b):
        where = piece(a, b)
        return remote(where, where, b_send, b_recv, sibling)

    half_of_all = all_of(wave, 8, b_send, b_recv)

    def gather(beside):
        for k in range(3):
            p_copy(k).start()
        q_copy(0, 0).start()
        q_copy(0, 1).start()
        to_sibling(p, q).start()
        beside()

        def column(j):
            p_arrival(j - 1).wait_recv()
            q_copy(j, 0).start()
            q_copy(j, 1).start()
            if j == 3:
                q_copy(j, 2).start()
            to_sibling(p + OFFSETS[j], q).start()

        def neighbours(j):
            for k in (0, 1):
                q_arrival(j, k).wait_recv()
                if j < 3:
                    q_copy(j, 2 + k).start()
            to_sibling(p + OFFSETS[j], q - 1).start()
            to_sibling(p + OFFSETS[j], q + 1).start()

        def opposite(j):
            q_arrival(j, 2).wait_recv()
            if j < 3:
                q_arrival(j, 3).wait_recv()
            to_sibling(p + OFFSETS[j], q + 2).start()

        column(1)
        column(2)
        neighbours(0)
        column(3)
        neighbours(1)
        neighbours(2)
        opposite(0)
        neighbours(3)
        opposite(1)
        opposite(2)
        opposite(3)
        half_of_all.wait_recv()

    def gather_sent():
        for k in range(3):
            p_copy(k).wait_send()
        all_of(wave, 6, q_send, b_recv).wait_send()
        half_of_all.wait_send()

    normaliser = 1.0 / math.sqrt(16 * TRIP)

    def compute(rows):
        live = count[0]
        for k in range(TRIP):
            weight = jnp.where(k < live, coef[triples[3, k]] * normaliser, 0.0)
            m = jnp.dot(
                left[triples[0, k], rows, :], wave[owner[triples[1, k]]], preferred_element_type=jnp.float32
            )
            mid[:, k * B : (k + 1) * B] = (m * weight).astype(jnp.bfloat16)
        rights = jnp.concatenate([right[triples[2, k]] for k in range(TRIP)], axis=0)
        return jnp.dot(mid[...], rights, preferred_element_type=jnp.float32)

    def rs_copy(dyl, dz):
        to = ((yl + dyl) % 2) * 8 + (z + dz) % 8
        return remote(pimg.at[to], rsbuf.at[term], r_send, r_recv, term_peer(dyl, dz))

    def spread(value):
        rows = jnp.sum(jnp.sum(value.reshape(-1, 8, B), axis=0), axis=0, keepdims=True)
        return rows[:, :128] + rows[:, 128:256] + rows[:, 256:]

    def sum_start(bufs, n, value):
        mine = bufs[0].at[term]
        mine[...] = jnp.concatenate(value + [jnp.zeros((1, 128), jnp.float32)] * (8 - len(value)), axis=0)
        for o in term_offsets:
            remote(mine, mine, s_send.at[n], s_recv.at[n], term_peer(*o)).start()

    def sum_forward(bufs, n):
        all_of(bufs[0], 15, s_send.at[n], s_recv.at[n]).wait_recv()
        mine = bufs[1].at[sector]
        mine[...] = jnp.sum(bufs[0][...], axis=0)
        for o in sector_offsets:
            remote(mine, mine, s_send.at[n + 1], s_recv.at[n + 1], sector_peer(*o)).start()

    def sum_finish(bufs, n):
        all_of(bufs[1], 15, s_send.at[n + 1], s_recv.at[n + 1]).wait_recv()
        return jnp.sum(jnp.sum(bufs[1][...], axis=0), axis=1, keepdims=True)

    def sum_sent(bufs, n):
        all_of(bufs[0], 15, s_send.at[n], s_recv.at[n]).wait_send()
        all_of(bufs[1], 15, s_send.at[n + 1], s_recv.at[n + 1]).wait_send()

    quotient_sum = (qabuf, qbbuf)
    norm_sum = (nabuf, nbbuf)

    def norm_scale(totals, quotient, i):
        ii, ic, ip, cc, cp, pp = [totals[j : j + 1] for j in range(6)]
        beta_now = beta[i]
        squares = (
            ii
            - 2.0 * quotient * ic
            - 2.0 * beta_now * ip
            + quotient * quotient * cc
            + 2.0 * quotient * beta_now * cp
            + beta_now * beta_now * pp
        )
        return 1.0 / jnp.sqrt(squares / (16 * B * B) + EPSILON)

    z_start()
    for move in moves[1:]:
        move.wait()
    z_all.wait_recv()
    z_all.wait_send()
    set_wave(zimg[...].astype(jnp.float32))
    own_rows = pl.ds(pl.multiple_of(PIECE * yl, 64), PIECE)
    other_rows = pl.ds(pl.multiple_of(PIECE * (1 - yl), 64), PIECE)
    share_rows = pl.ds(pl.multiple_of(SHARE * z, 8), SHARE)

    def application(i, carry):
        def beside():
            @pl.when(i == 0)
            def _():
                state_start()

            @pl.when(i > 0)
            def _():
                sum_forward(norm_sum, 2)

        gather(beside)

        @pl.when(i > 0)
        def _():
            scale[...] = norm_scale(sum_finish(norm_sum, 2), ray_now[...], i - 1)

        factor = scale[...]
        applied = compute(other_rows) * factor
        overlap = spread(wave[sector, other_rows, :].astype(jnp.float32) * applied)
        pimg[pl.ds((1 - yl) * 8, 8)] = applied.reshape(8, SHARE, B).astype(jnp.bfloat16)
        for dz in ring + (0,):
            rs_copy(1, dz).start()
        gather_sent()
        applied = compute(own_rows) * factor
        img[...] = applied
        overlap = overlap + spread(wave[sector, own_rows, :].astype(jnp.float32) * applied)
        now = cur[...] * factor

        @pl.when(i < APPS - 1)
        def _():
            sum_start(quotient_sum, 0, [overlap * factor, spread(now * now)])

        pimg[pl.ds(yl * 8, 8)] = applied.reshape(8, SHARE, B).astype(jnp.bfloat16)
        for dz in ring:
            rs_copy(0, dz).start()
        rsbuf[term] = jnp.zeros((SHARE, B), jnp.bfloat16)

        @pl.when(i == 0)
        def _():
            state_finish()

        @pl.when(i > 0)
        def _():
            sum_sent(norm_sum, 2)
            zcur[...] = zcur[...] * factor

        before = prev[...]
        square = diag[...] * diag[...]
        squared_now = square * now
        squared_before = square * before
        fixed = [spread(squared_now * now), spread(squared_now * before), spread(squared_before * before)]

        @pl.when(i < APPS - 1)
        def _():
            sum_forward(quotient_sum, 0)

        all_of(rsbuf, 15, r_send, r_recv).wait_recv()
        image = img[share_rows, :]
        for t in range(16):
            image = image + rsbuf[t].astype(jnp.float32)

        @pl.when(i < APPS - 1)
        def _():
            zimg[z] = image.astype(jnp.bfloat16)
            z_start()

        squared_image = square * image
        values = [spread(squared_image * image), spread(squared_now * image), spread(squared_before * image)]
        values += fixed + [spread(now * image), spread(now * now)]

        @pl.when(i < APPS - 1)
        def _():
            sum_start(norm_sum, 2, values)

        @pl.when(i == APPS - 1)
        def _():
            sum_start(quotient_sum, 0, values)

        all_of(pimg, 15, r_send, r_recv).wait_send()
        cur[...] = now
        last[...] = image

        @pl.when(i < APPS - 1)
        def _():
            totals = sum_finish(quotient_sum, 0)
            quotient = totals[0:1] / totals[1:2]
            ray_now[...] = quotient
            beta_now = beta[i]
            z_all.wait_recv()
            znow = zcur[...]
            znext = zdiag[...] * (zimg[...].astype(jnp.float32) - quotient * znow - beta_now * zprev[...])
            set_wave(znext)
            zprev[...] = znow
            zcur[...] = znext
            z_all.wait_send()

            cur[...] = diag[...] * (image - quotient * now - beta_now * before)
            prev[...] = now
            ray_ref[i] = jnp.sum(quotient)
            sum_sent(quotient_sum, 0)

        return carry

    lax.fori_loop(0, APPS, application, 0)
    sum_forward(quotient_sum, 0)
    totals = sum_finish(quotient_sum, 0)
    quotient = totals[6:7] / totals[7:8]
    residual = diag[...] * (last[...] - quotient * cur[...] - beta[APPS - 1] * prev[...])
    out_ref[0] = residual * norm_scale(totals, quotient, APPS - 1)
    ray_ref[APPS - 1] = jnp.sum(quotient)
    sum_sent(quotient_sum, 0)


def local(x_start, x_prev, precond, left_env, right_env, triples, trip_count, term_coef, lanczos_beta, block_owner):
    vmem = pl.BlockSpec(memory_space=pltpu.VMEM)
    smem = pl.BlockSpec(memory_space=pltpu.SMEM)
    hbm = pl.BlockSpec(memory_space=pltpu.HBM)
    dma = pltpu.SemaphoreType.DMA
    f32, bf16 = jnp.float32, jnp.bfloat16
    return pl.pallas_call(
        kernel,
        out_shape=(jax.ShapeDtypeStruct((1, SHARE, B), f32), jax.ShapeDtypeStruct((APPS,), f32)),
        in_specs=[hbm] * 10,
        out_specs=(vmem, smem),
        scratch_shapes=[
            pltpu.VMEM((8, B, B), bf16),
            pltpu.VMEM((8, B, B), bf16),
            pltpu.VMEM((16, B, B), bf16),
            pltpu.VMEM((PIECE, TRIP * B), bf16),
            pltpu.VMEM((PIECE, B), f32),
            pltpu.VMEM((16, SHARE, B), bf16),
            pltpu.VMEM((16, SHARE, B), bf16),
            pltpu.VMEM((8, SHARE, B), bf16),
            pltpu.VMEM((8, SHARE, B), f32),
            pltpu.VMEM((8, SHARE, B), f32),
            pltpu.VMEM((8, SHARE, B), f32),
            pltpu.VMEM((1, 1), f32),
            pltpu.VMEM((1, 1), f32),
            pltpu.VMEM((SHARE, B), f32),
            pltpu.VMEM((SHARE, B), f32),
            pltpu.VMEM((SHARE, B), f32),
            pltpu.VMEM((SHARE, B), f32),
            pltpu.VMEM((16, 8, 128), f32),
            pltpu.VMEM((16, 8, 128), f32),
            pltpu.VMEM((16, 8, 128), f32),
            pltpu.VMEM((16, 8, 128), f32),
            pltpu.SMEM((4, TRIP), jnp.int32),
            pltpu.SMEM((1,), jnp.int32),
            pltpu.SMEM((64,), f32),
            pltpu.SMEM((APPS,), f32),
            pltpu.SMEM((16,), jnp.int32),
            dma((10,)),
            dma((3,)),
            dma((19,)),
            dma,
            dma,
            dma,
            dma,
            dma,
            dma,
            dma,
            dma((4,)),
            dma((4,)),
            dma((3,)),
            dma((3,)),
        ],
        compiler_params=pltpu.CompilerParams(
            collective_id=0, has_side_effects=True, vmem_limit_bytes=64 * 2**20
        ),
        name="window",
    )(x_start, x_prev, precond, left_env, right_env, triples.T, trip_count.reshape(1), term_coef, lanczos_beta, block_owner)


def solution(mesh):
    torus = Mesh(mesh.devices.reshape(4, 2, 2, 2, 8), ALL)
    return jax.shard_map(
        local,
        mesh=torus,
        in_specs=(
            P(SECTOR, TERM, None),
            P(SECTOR, TERM, None),
            P(SECTOR, TERM, None),
            P(ALL, None, None),
            P(ALL, None, None),
            P(ALL, None),
            P(SECTOR, TERM),
            P(),
            P(),
            P(),
        ),
        out_specs=(P(SECTOR, TERM, None), P()),
        check_vma=False,
    )
```

```python
import math

import jax
import jax.numpy as jnp
from jax import lax
from jax.experimental import pallas as pl
from jax.experimental.pallas import tpu as pltpu
from jax.sharding import Mesh
from jax.sharding import PartitionSpec as P

APPS = 3
B = 384
TRIP = 20
SHARE = 24
PIECE = 192
HALF = 96
SECTOR = ("x", "yh", "c")
TERM = ("yl", "z")
ALL = ("x", "yh", "c", "yl", "z")
EPSILON = 1e-06
MESH = pl.DeviceIdType.MESH
OFFSETS = (0, -1, 1, 2)


def kernel(
    x_hbm,
    xp_hbm,
    d_hbm,
    left_hbm,
    right_hbm,
    triples_hbm,
    count_hbm,
    coef_hbm,
    beta_hbm,
    owner_hbm,
    out_ref,
    ray_ref,
    left,
    right,
    wave,
    mid,
    img,
    pimg,
    rsbuf,
    zimg,
    zcur,
    zprev,
    zdiag,
    scale,
    ray_now,
    cur,
    prev,
    diag,
    last,
    qabuf,
    qbbuf,
    nabuf,
    nbbuf,
    triples,
    count,
    coef,
    beta,
    owner,
    in_sem,
    g_send,
    g_recv,
    q_send,
    b_send,
    b_recv,
    r_send,
    r_recv,
    z_send,
    z_recv,
    s_send,
    s_recv,
    i_send,
    i_recv,
):
    x = lax.axis_index("x")
    yh = lax.axis_index("yh")
    c = lax.axis_index("c")
    yl = lax.axis_index("yl")
    z = lax.axis_index("z")
    y = yh * 2 + yl
    sector = (x * 2 + yh) * 2 + c
    term = yl * 8 + z
    p = (1 - c) * y + c * x
    q = (1 - c) * x + c * y

    def device(nx, ny, nc, nz):
        return {"x": nx, "yh": ny // 2, "c": nc, "yl": ny % 2, "z": nz}

    def along_p(d):
        return device((x + c * d + 4) % 4, (y + (1 - c) * d + 4) % 4, c, z)

    def along_q(d):
        return device((x + (1 - c) * d + 4) % 4, (y + c * d + 4) % 4, c, z)

    def term_peer(dyl, dz):
        return {"x": x, "yh": yh, "c": c, "yl": (yl + dyl) % 2, "z": (z + dz) % 8}

    def sector_peer(dx, dyh, dc):
        return {"x": (x + dx) % 4, "yh": (yh + dyh) % 2, "c": (c + dc) % 2, "yl": yl, "z": z}

    ring = (4, 3, 5, 2, 6, 1, 7)
    term_offsets = [(1, 4), (1, 3), (1, 5), (0, 4)] + [(1, 2), (1, 6), (0, 3), (0, 5), (1, 1), (1, 7)]
    term_offsets += [(0, 2), (0, 6), (1, 0), (0, 1), (0, 7)]
    sector_offsets = [(2, 1, 0), (2, 1, 1), (1, 1, 0), (1, 1, 1), (3, 1, 0), (3, 1, 1), (2, 0, 0), (2, 0, 1)]
    sector_offsets += [(0, 1, 0), (0, 1, 1), (1, 0, 0), (1, 0, 1), (3, 0, 0), (3, 0, 1), (0, 0, 1)]
    sibling = sector_peer(0, 0, 1)

    def remote(src, dst, send, recv, dev):
        return pltpu.make_async_remote_copy(
            src_ref=src, dst_ref=dst, send_sem=send, recv_sem=recv, device_id=dev, device_id_type=MESH
        )

    moves = [
        pltpu.make_async_copy(src, dst, in_sem.at[n])
        for n, (src, dst) in enumerate(
            (
                (x_hbm.at[0], cur),
                (xp_hbm.at[0], prev),
                (d_hbm.at[0], diag),
                (triples_hbm, triples),
                (count_hbm, count),
                (coef_hbm, coef),
                (beta_hbm, beta),
                (owner_hbm, owner),
                (left_hbm, left),
                (right_hbm, right),
            )
        )
    ]
    for move in moves:
        move.start()

    barrier = pltpu.get_barrier_semaphore()
    peers = [term_peer(0, dz) for dz in ring] + [along_p(1), along_p(-1), along_p(2)]
    peers += [along_q(1), along_q(-1), sibling]
    for dev in peers:
        pl.semaphore_signal(barrier, inc=1, device_id=dev, device_id_type=MESH)
    moves[0].wait()
    zimg[z] = cur[...].astype(jnp.bfloat16)
    scale[...] = jnp.ones_like(scale)
    pl.semaphore_wait(barrier, len(peers))

    def z_copy(dz):
        mine = zimg.at[z]
        return remote(mine, mine, z_send, z_recv, term_peer(0, dz))

    def all_of(ref, length, send, recv):
        return remote(ref.at[pl.ds(0, length)], ref.at[pl.ds(0, length)], send, recv, sibling)

    z_all = all_of(zimg, 7, z_send, z_recv)

    def z_start():
        for dz in ring:
            z_copy(dz).start()

    def set_wave(value):
        rows = pl.ds(pl.multiple_of(PIECE * yl, 64), PIECE)
        wave[sector, rows, :] = value.reshape(PIECE, B).astype(jnp.bfloat16)

    states = ((0, zcur), (1, zprev), (2, zdiag))

    def state_copy(n, dz):
        mine = states[n][1].at[z]
        return remote(mine, mine, i_send.at[n], i_recv.at[n], term_peer(0, dz))

    def state_start():
        for n, own in enumerate((cur, prev, diag)):
            states[n][1][z] = own[...]
            for dz in ring:
                state_copy(n, dz).start()

    def state_finish():
        for n in range(3):
            everything = all_of(states[n][1], 7, i_send.at[n], i_recv.at[n])
            everything.wait_recv()
            everything.wait_send()

    def piece_at(px, py, core, start, length):
        block = (px * 2 + py // 2) * 2 + core
        rows = pl.multiple_of((py % 2) * PIECE + start, 32)
        return wave.at[block, pl.ds(rows, length)]

    def piece(a, b, start=0, length=PIECE):
        a, b = (a + 4) % 4, (b + 4) % 4
        return piece_at((1 - c) * b + c * a, (1 - c) * a + c * b, c, start, length)

    def p_copy(k):
        where = piece(p, q)
        return remote(where, where, g_send.at[k], g_recv.at[k], along_p((1, -1, 2)[k]))

    def p_arrival(k):
        where = piece(p - (1, -1, 2)[k], q)
        return remote(where, where, g_send.at[k], g_recv.at[k], along_p((1, -1, 2)[k]))

    def q_copy(j, k):
        a = p + OFFSETS[j]
        where = (piece(a, q), piece(a, q), piece(a, q - 1, 0, HALF), piece(a, q + 1, HALF, HALF))[k]
        dev = along_q(1 if k % 2 == 0 else -1)
        n = 3 + 4 * j + k
        if j == 3 and k == 2:
            where, dev = piece(a, q), along_q(2)
        return remote(where, where, q_send, g_recv.at[n], dev)

    def q_arrival(j, k):
        a = p + OFFSETS[j]
        where = (piece(a, q - 1), piece(a, q + 1), piece(a, q - 2, 0, HALF), piece(a, q + 2, HALF, HALF))[k]
        dev = along_q(1 if k % 2 == 0 else -1)
        n = 3 + 4 * j + k
        if j == 3 and k == 2:
            where, dev = piece(a, q - 2), along_q(2)
        return remote(where, where, q_send, g_recv.at[n], dev)

    def to_sibling(a, b):
        where = piece(a, b)
        return remote(where, where, b_send, b_recv, sibling)

    half_of_all = all_of(wave, 8, b_send, b_recv)

    def gather(beside):
        for k in range(3):
            p_copy(k).start()
        q_copy(0, 0).start()
        q_copy(0, 1).start()
        to_sibling(p, q).start()

        def column(j):
            p_arrival(j - 1).wait_recv()
            q_copy(j, 0).start()
            q_copy(j, 1).start()
            if j == 3:
                q_copy(j, 2).start()
            to_sibling(p + OFFSETS[j], q).start()

        def neighbours(j):
            for k in (0, 1):
                q_arrival(j, k).wait_recv()
                if j < 3:
                    q_copy(j, 2 + k).start()
            to_sibling(p + OFFSETS[j], q - 1).start()
            to_sibling(p + OFFSETS[j], q + 1).start()

        def opposite(j):
            q_arrival(j, 2).wait_recv()
            if j < 3:
                q_arrival(j, 3).wait_recv()
            to_sibling(p + OFFSETS[j], q + 2).start()

        column(1)
        column(2)
        beside()
        neighbours(0)
        column(3)
        neighbours(1)
        neighbours(2)
        opposite(0)
        neighbours(3)
        opposite(1)
        opposite(2)
        opposite(3)
        half_of_all.wait_recv()

    def gather_sent():
        for k in range(3):
            p_copy(k).wait_send()
        all_of(wave, 6, q_send, b_recv).wait_send()
        half_of_all.wait_send()

    normaliser = 1.0 / math.sqrt(16 * TRIP)

    def compute(rows):
        live = count[0]
        for k in range(TRIP):
            weight = jnp.where(k < live, coef[triples[3, k]] * normaliser, 0.0)
            m = jnp.dot(
                left[triples[0, k], rows, :], wave[owner[triples[1, k]]], preferred_element_type=jnp.float32
            )
            mid[:, k * B : (k + 1) * B] = (m * weight).astype(jnp.bfloat16)
        rights = jnp.concatenate([right[triples[2, k]] for k in range(TRIP)], axis=0)
        return jnp.dot(mid[...], rights, preferred_element_type=jnp.float32)

    def rs_copy(dyl, dz):
        to = ((yl + dyl) % 2) * 8 + (z + dz) % 8
        return remote(pimg.at[to], rsbuf.at[term], r_send, r_recv, term_peer(dyl, dz))

    def spread(value):
        rows = jnp.sum(jnp.sum(value.reshape(-1, 8, B), axis=0), axis=0, keepdims=True)
        return rows[:, :128] + rows[:, 128:256] + rows[:, 256:]

    def sum_start(bufs, n, value):
        mine = bufs[0].at[term]
        mine[...] = jnp.concatenate(value + [jnp.zeros((1, 128), jnp.float32)] * (8 - len(value)), axis=0)
        for o in term_offsets:
            remote(mine, mine, s_send.at[n], s_recv.at[n], term_peer(*o)).start()

    def sum_forward(bufs, n):
        all_of(bufs[0], 15, s_send.at[n], s_recv.at[n]).wait_recv()
        mine = bufs[1].at[sector]
        mine[...] = jnp.sum(bufs[0][...], axis=0)
        for o in sector_offsets:
            remote(mine, mine, s_send.at[n + 1], s_recv.at[n + 1], sector_peer(*o)).start()

    def sum_finish(bufs, n):
        all_of(bufs[1], 15, s_send.at[n + 1], s_recv.at[n + 1]).wait_recv()
        return jnp.sum(jnp.sum(bufs[1][...], axis=0), axis=1, keepdims=True)

    def sum_sent(bufs, n):
        all_of(bufs[0], 15, s_send.at[n], s_recv.at[n]).wait_send()
        all_of(bufs[1], 15, s_send.at[n + 1], s_recv.at[n + 1]).wait_send()

    quotient_sum = (qabuf, qbbuf)
    norm_sum = (nabuf, nbbuf)

    def norm_scale(totals, quotient, i):
        ii, ic, ip, cc, cp, pp = [totals[j : j + 1] for j in range(6)]
        beta_now = beta[i]
        squares = (
            ii
            - 2.0 * quotient * ic
            - 2.0 * beta_now * ip
            + quotient * quotient * cc
            + 2.0 * quotient * beta_now * cp
            + beta_now * beta_now * pp
        )
        return 1.0 / jnp.sqrt(squares / (16 * B * B) + EPSILON)

    z_start()
    for move in moves[1:]:
        move.wait()
    z_all.wait_recv()
    z_all.wait_send()
    set_wave(zimg[...].astype(jnp.float32))
    own_rows = pl.ds(pl.multiple_of(PIECE * yl, 64), PIECE)
    other_rows = pl.ds(pl.multiple_of(PIECE * (1 - yl), 64), PIECE)
    share_rows = pl.ds(pl.multiple_of(SHARE * z, 8), SHARE)

    def application(i, carry):
        def beside():
            @pl.when(i == 0)
            def _():
                state_start()

            @pl.when(i > 0)
            def _():
                sum_forward(norm_sum, 2)

        gather(beside)

        @pl.when(i > 0)
        def _():
            scale[...] = norm_scale(sum_finish(norm_sum, 2), ray_now[...], i - 1)

        factor = scale[...]
        applied = compute(other_rows) * factor
        overlap = spread(wave[sector, other_rows, :].astype(jnp.float32) * applied)
        pimg[pl.ds((1 - yl) * 8, 8)] = applied.reshape(8, SHARE, B).astype(jnp.bfloat16)
        for dz in ring + (0,):
            rs_copy(1, dz).start()
        gather_sent()
        applied = compute(own_rows) * factor
        img[...] = applied
        overlap = overlap + spread(wave[sector, own_rows, :].astype(jnp.float32) * applied)
        now = cur[...] * factor

        @pl.when(i < APPS - 1)
        def _():
            sum_start(quotient_sum, 0, [overlap * factor, spread(now * now)])

        pimg[pl.ds(yl * 8, 8)] = applied.reshape(8, SHARE, B).astype(jnp.bfloat16)
        for dz in ring:
            rs_copy(0, dz).start()
        rsbuf[term] = jnp.zeros((SHARE, B), jnp.bfloat16)

        @pl.when(i == 0)
        def _():
            state_finish()

        @pl.when(i > 0)
        def _():
            sum_sent(norm_sum, 2)
            zcur[...] = zcur[...] * factor

        before = prev[...]
        square = diag[...] * diag[...]
        squared_now = square * now
        squared_before = square * before
        fixed = [spread(squared_now * now), spread(squared_now * before), spread(squared_before * before)]

        @pl.when(i < APPS - 1)
        def _():
            sum_forward(quotient_sum, 0)

        all_of(rsbuf, 15, r_send, r_recv).wait_recv()
        image = img[share_rows, :]
        for t in range(16):
            image = image + rsbuf[t].astype(jnp.float32)

        @pl.when(i < APPS - 1)
        def _():
            zimg[z] = image.astype(jnp.bfloat16)
            z_start()

        squared_image = square * image
        values = [spread(squared_image * image), spread(squared_now * image), spread(squared_before * image)]
        values += fixed + [spread(now * image), spread(now * now)]

        @pl.when(i < APPS - 1)
        def _():
            sum_start(norm_sum, 2, values)

        @pl.when(i == APPS - 1)
        def _():
            sum_start(quotient_sum, 0, values)

        all_of(pimg, 15, r_send, r_recv).wait_send()
        cur[...] = now
        last[...] = image

        @pl.when(i < APPS - 1)
        def _():
            totals = sum_finish(quotient_sum, 0)
            quotient = totals[0:1] / totals[1:2]
            ray_now[...] = quotient
            beta_now = beta[i]
            z_all.wait_recv()
            znow = zcur[...]
            znext = zdiag[...] * (zimg[...].astype(jnp.float32) - quotient * znow - beta_now * zprev[...])
            set_wave(znext)
            zprev[...] = znow
            zcur[...] = znext
            z_all.wait_send()

            cur[...] = diag[...] * (image - quotient * now - beta_now * before)
            prev[...] = now
            ray_ref[i] = jnp.sum(quotient)
            sum_sent(quotient_sum, 0)

        return carry

    lax.fori_loop(0, APPS, application, 0)
    sum_forward(quotient_sum, 0)
    totals = sum_finish(quotient_sum, 0)
    quotient = totals[6:7] / totals[7:8]
    residual = diag[...] * (last[...] - quotient * cur[...] - beta[APPS - 1] * prev[...])
    out_ref[0] = residual * norm_scale(totals, quotient, APPS - 1)
    ray_ref[APPS - 1] = jnp.sum(quotient)
    sum_sent(quotient_sum, 0)


def local(x_start, x_prev, precond, left_env, right_env, triples, trip_count, term_coef, lanczos_beta, block_owner):
    vmem = pl.BlockSpec(memory_space=pltpu.VMEM)
    smem = pl.BlockSpec(memory_space=pltpu.SMEM)
    hbm = pl.BlockSpec(memory_space=pltpu.HBM)
    dma = pltpu.SemaphoreType.DMA
    f32, bf16 = jnp.float32, jnp.bfloat16
    return pl.pallas_call(
        kernel,
        out_shape=(jax.ShapeDtypeStruct((1, SHARE, B), f32), jax.ShapeDtypeStruct((APPS,), f32)),
        in_specs=[hbm] * 10,
        out_specs=(vmem, smem),
        scratch_shapes=[
            pltpu.VMEM((8, B, B), bf16),
            pltpu.VMEM((8, B, B), bf16),
            pltpu.VMEM((16, B, B), bf16),
            pltpu.VMEM((PIECE, TRIP * B), bf16),
            pltpu.VMEM((PIECE, B), f32),
            pltpu.VMEM((16, SHARE, B), bf16),
            pltpu.VMEM((16, SHARE, B), bf16),
            pltpu.VMEM((8, SHARE, B), bf16),
            pltpu.VMEM((8, SHARE, B), f32),
            pltpu.VMEM((8, SHARE, B), f32),
            pltpu.VMEM((8, SHARE, B), f32),
            pltpu.VMEM((1, 1), f32),
            pltpu.VMEM((1, 1), f32),
            pltpu.VMEM((SHARE, B), f32),
            pltpu.VMEM((SHARE, B), f32),
            pltpu.VMEM((SHARE, B), f32),
            pltpu.VMEM((SHARE, B), f32),
            pltpu.VMEM((16, 8, 128), f32),
            pltpu.VMEM((16, 8, 128), f32),
            pltpu.VMEM((16, 8, 128), f32),
            pltpu.VMEM((16, 8, 128), f32),
            pltpu.SMEM((4, TRIP), jnp.int32),
            pltpu.SMEM((1,), jnp.int32),
            pltpu.SMEM((64,), f32),
            pltpu.SMEM((APPS,), f32),
            pltpu.SMEM((16,), jnp.int32),
            dma((10,)),
            dma((3,)),
            dma((19,)),
            dma,
            dma,
            dma,
            dma,
            dma,
            dma,
            dma,
            dma((4,)),
            dma((4,)),
            dma((3,)),
            dma((3,)),
        ],
        compiler_params=pltpu.CompilerParams(
            collective_id=0, has_side_effects=True, vmem_limit_bytes=64 * 2**20
        ),
        name="window",
    )(x_start, x_prev, precond, left_env, right_env, triples.T, trip_count.reshape(1), term_coef, lanczos_beta, block_owner)


def solution(mesh):
    torus = Mesh(mesh.devices.reshape(4, 2, 2, 2, 8), ALL)
    return jax.shard_map(
        local,
        mesh=torus,
        in_specs=(
            P(SECTOR, TERM, None),
            P(SECTOR, TERM, None),
            P(SECTOR, TERM, None),
            P(ALL, None, None),
            P(ALL, None, None),
            P(ALL, None),
            P(SECTOR, TERM),
            P(),
            P(),
            P(),
        ),
        out_specs=(P(SECTOR, TERM, None), P()),
        check_vma=False,
    )
```
